256 devices in a mesh: dp: 2 (over core), row: 16 (over z_lo, y), col: 8 (over z_hi, x).
Axes of the slice: x: 4, y: 4, z: 8 (z_hi: 2, z_lo: 4; z = z_hi * 4 + z_lo), core: 2. Of those that a mesh axis runs over, the one named last changes fastest.
Arguments:
- features: bfloat16 [2, 64, 256, 2048], P('dp', None, 'row', 'col'), may hold values from -6 to 6
- grad_out: bfloat16 [2, 64, 256, 2048], P('dp', None, 'row', 'col'), may hold values from -6 to 6
- kernel_one: bfloat16 [3, 3, 64, 64], replicated, may hold values from -0.25 to 0.25
- kernel_two: bfloat16 [3, 3, 64, 64], replicated, may hold values from -0.25 to 0.25
Outputs:
- grad_features: bfloat16 [2, 64, 256, 2048], P('dp', None, 'row', 'col')
- grad_kernel_one: float32 [3, 3, 64, 64], replicated
- grad_kernel_two: float32 [3, 3, 64, 64], replicated
The draws below stay inside these ranges and needn't reach their ends.
All inputs are finite; a program needn't handle non-finite values.
Results may differ from the reference program's by a relative error of at most 0.0061.
Values may be sent and summed in bfloat16 or wider, within the bound.
A program may use at most 64 MiB of HBM per device.

```python
import jax
import jax.numpy as jnp
from jax import lax

C = 64
BATCH = 2
NH = 256
NW = 2048


def level_of(own_key, shape, pieces, smallest, top_value):
    loudness, own = 1.0, jax.random.fold_in(own_key, 6)
    for axis_at, shards_of in pieces:
        steps = jnp.exp(jax.random.uniform(jax.random.fold_in(own, axis_at), (shards_of,), jnp.float32, smallest / len(pieces), top_value / len(pieces)))
        loudness = loudness * jnp.repeat(steps, shape[axis_at] // shards_of).reshape([-1 if axis == axis_at else 1 for axis in range(len(shape))])
    return loudness


def centred(key, shape, spread, most, split=(), dtype=jnp.bfloat16):
    gain = level_of(key, shape, split, -0.22, 0.18) if split else 1.0
    drawn = jax.random.normal(key, shape, jnp.float32) * spread * gain
    return jnp.minimum(jnp.maximum(drawn, -most), most).astype(dtype)


def setup_inputs(seed: int = 0) -> dict:
    streams_of = jax.random.split(jax.random.key(seed), 5)
    features = centred(streams_of[0], (BATCH, C, NH, NW), 1.0, 6.0, ((0, 2), (2, 16), (3, 8)))
    grad_out = centred(streams_of[1], (BATCH, C, NH, NW), 1.0, 6.0, ((0, 2), (2, 16), (3, 8)))
    kernel_one = centred(streams_of[2], (3, 3, C, C), (9 * C) ** -0.5, 0.25)
    kernel_two = centred(streams_of[3], (3, 3, C, C), (9 * C) ** -0.5, 0.25)
    return dict(features=features, grad_out=grad_out, kernel_one=kernel_one, kernel_two=kernel_two)


def convolve(padded, kernel, rows, cols):
    total = jnp.zeros((padded.shape[0], kernel.shape[2], rows, cols), jnp.float32)
    for ky in range(3):
        for kx in range(3):
            total = total + jnp.einsum('oi,sihw->sohw', kernel[ky, kx].astype(jnp.float32), padded[:, :, ky:ky + rows, kx:kx + cols].astype(jnp.float32), precision=lax.Precision.HIGHEST)
    return total

def transposed(padded, kernel, rows, cols):
    total = jnp.zeros((padded.shape[0], kernel.shape[3], rows, cols), jnp.float32)
    for ky in range(3):
        for kx in range(3):
            total = total + jnp.einsum('oi,sohw->sihw', kernel[ky, kx].astype(jnp.float32), padded[:, :, 2 - ky:2 - ky + rows, 2 - kx:2 - kx + cols].astype(jnp.float32), precision=lax.Precision.HIGHEST)
    return total

def kernel_grad(padded, delta, rows, cols):
    taps = []
    for ky in range(3):
        line = []
        for kx in range(3):
            line.append(jnp.einsum('sohw,sihw->oi', delta.astype(jnp.float32), padded[:, :, ky:ky + rows, kx:kx + cols].astype(jnp.float32), precision=lax.Precision.HIGHEST))
        taps.append(jnp.stack(line))
    return jnp.stack(taps)

def dsilu(value):
    sig = jax.nn.sigmoid(value)
    return sig * (1.0 + value * (1.0 - sig))

def padding(value):
    return jnp.pad(value, ((0, 0), (0, 0), (1, 1), (1, 1)))

def reference(features, grad_out, kernel_one, kernel_two):
    rows, cols = (features.shape[2], features.shape[3])
    feat_pad = padding(features)
    pre_one = convolve(feat_pad, kernel_one, rows, cols)
    hidden = jax.nn.silu(pre_one).astype(jnp.bfloat16)
    hid_pad = padding(hidden)
    pre_two = convolve(hid_pad, kernel_two, rows, cols)
    delta_two = (grad_out.astype(jnp.float32) * dsilu(pre_two)).astype(jnp.bfloat16)
    back_one = transposed(padding(delta_two), kernel_two, rows, cols)
    delta_one = (back_one * dsilu(pre_one)).astype(jnp.bfloat16)
    grad_features = transposed(padding(delta_one), kernel_one, rows, cols).astype(jnp.bfloat16)
    scale = 1.0 / jnp.sqrt(jnp.float32(features.shape[0] * rows * cols))
    grad_two = kernel_grad(hid_pad, delta_two, rows, cols) * scale
    grad_one = kernel_grad(feat_pad, delta_one, rows, cols) * scale
    return (grad_features, grad_one, grad_two)
```

```python
import functools
import jax
import jax.numpy as jnp
from jax import lax
from jax.experimental import pallas as pl
from jax.experimental.pallas import tpu as pltpu
from jax.sharding import PartitionSpec as P

MESH = pl.DeviceIdType.MESH


def reduce_kernel(plane, depth, near_row, near_col, mine_ref, out_ref, landed, part, stacked, final, gathered,
                  scatter_send, scatter_recv, depth_send, depth_recv, gather_send, gather_recv):
    dp, row, col = lax.axis_index("dp"), lax.axis_index("row"), lax.axis_index("col")
    far_row, far_col = row // near_row, col // near_col
    me = (dp * near_row + row % near_row) * near_col + col % near_col
    layer = far_col * (lax.axis_size("row") // near_row) + far_row

    def in_plane(member):
        return (member // (near_row * near_col), far_row * near_row + member // near_col % near_row, far_col * near_col + member % near_col)

    def in_depth(step):
        other = (layer + step) % depth
        rows = lax.axis_size("row") // near_row
        return (dp, other % rows * near_row + row % near_row, other // rows * near_col + col % near_col)

    barrier = pltpu.get_barrier_semaphore()

    def greet(step, carry):
        pl.semaphore_signal(barrier, inc=1, device_id=in_plane((me + step) % plane), device_id_type=MESH)
        return carry

    def greet_depth(step, carry):
        pl.semaphore_signal(barrier, inc=1, device_id=in_depth(step), device_id_type=MESH)
        return carry

    lax.fori_loop(1, plane, greet, 0)
    lax.fori_loop(1, depth, greet_depth, 0)
    pl.semaphore_wait(barrier, plane + depth - 2)

    def scatter(step):
        other = (me + step) % plane
        return pltpu.make_async_remote_copy(
            src_ref=mine_ref.at[other], dst_ref=landed.at[step - 1], send_sem=scatter_send, recv_sem=scatter_recv,
            device_id=in_plane(other), device_id_type=MESH)

    def start_scatter(step, carry):
        scatter(step).start()
        return carry

    lax.fori_loop(1, plane, start_scatter, 0)
    pltpu.make_async_copy(landed, landed, scatter_recv).wait()
    part[...] = mine_ref[me] + jnp.sum(landed[...], axis=0)
    stacked[layer] = part[...]

    def start_depth(step, carry):
        pltpu.make_async_remote_copy(
            src_ref=part, dst_ref=stacked.at[layer], send_sem=depth_send, recv_sem=depth_recv,
            device_id=in_depth(step), device_id_type=MESH).start()
        return carry

    lax.fori_loop(1, depth, start_depth, 0)
    others = stacked.at[pl.ds(0, depth - 1)]
    pltpu.make_async_copy(others, others, depth_recv).wait()
    final[...] = jnp.sum(stacked[...], axis=0)
    gathered[me] = final[...]

    def start_gather(step, carry):
        pltpu.make_async_remote_copy(
            src_ref=final, dst_ref=gathered.at[me], send_sem=gather_send, recv_sem=gather_recv,
            device_id=in_plane((me + step) % plane), device_id_type=MESH).start()
        return carry

    lax.fori_loop(1, plane, start_gather, 0)
    members = gathered.at[pl.ds(0, plane - 1)]
    pltpu.make_async_copy(members, members, gather_recv).wait()
    out_ref[...] = gathered[...]
    pltpu.make_async_copy(landed, landed, scatter_send).wait()
    pltpu.make_async_copy(others, others, depth_send).wait()
    pltpu.make_async_copy(members, members, gather_send).wait()


def summed(values):
    near_row, near_col = 4, 4
    plane = lax.axis_size("dp") * near_row * near_col
    depth = lax.axis_size("row") // near_row * (lax.axis_size("col") // near_col)
    chunk = values.size // plane // 128
    return pl.pallas_call(
        functools.partial(reduce_kernel, plane, depth, near_row, near_col),
        out_shape=jax.ShapeDtypeStruct((plane, chunk, 128), jnp.float32),
        in_specs=[pl.BlockSpec(memory_space=pltpu.VMEM)],
        out_specs=pl.BlockSpec(memory_space=pltpu.VMEM),
        scratch_shapes=[
            pltpu.VMEM((plane - 1, chunk, 128), jnp.float32),
            pltpu.VMEM((chunk, 128), jnp.float32),
            pltpu.VMEM((depth, chunk, 128), jnp.float32),
            pltpu.VMEM((chunk, 128), jnp.float32),
            pltpu.VMEM((plane, chunk, 128), jnp.float32),
        ] + [pltpu.SemaphoreType.DMA] * 6,
        compiler_params=pltpu.CompilerParams(collective_id=0, has_side_effects=True),
    )(values.reshape(plane, chunk, 128))


def extended(cells, sides, width):
    for axis, dim in sides:
        count = lax.axis_size(axis)
        ends = count - 1
        head = lax.slice_in_dim(cells, 0, width, axis=dim)
        tail = lax.slice_in_dim(cells, cells.shape[dim] - width, cells.shape[dim], axis=dim)
        cells = jnp.concatenate(
            [
                lax.ppermute(tail, axis, [(i, (i + 1) % count) for i in range(ends)]),
                cells,
                lax.ppermute(head, axis, [((i + 1) % count, i) for i in range(ends)]),
            ],
            axis=dim,
        )
    return cells


def convolve(padded, kernel, rows, cols):
    total = jnp.zeros((padded.shape[0], kernel.shape[2], rows, cols), jnp.float32)
    for ky in range(3):
        for kx in range(3):
            total = total + jnp.einsum(
                "oi,sihw->sohw",
                kernel[ky, kx],
                padded[:, :, ky : ky + rows, kx : kx + cols],
                preferred_element_type=jnp.float32,
            )
    return total


def transposed(padded, kernel, rows, cols):
    total = jnp.zeros((padded.shape[0], kernel.shape[3], rows, cols), jnp.float32)
    for ky in range(3):
        for kx in range(3):
            total = total + jnp.einsum(
                "oi,sohw->sihw",
                kernel[ky, kx],
                padded[:, :, 2 - ky : 2 - ky + rows, 2 - kx : 2 - kx + cols],
                preferred_element_type=jnp.float32,
            )
    return total


def kernel_grad(padded, delta, rows, cols):
    taps = []
    for ky in range(3):
        line = []
        for kx in range(3):
            line.append(
                jnp.einsum(
                    "sohw,sihw->oi",
                    delta,
                    padded[:, :, ky : ky + rows, kx : kx + cols],
                    preferred_element_type=jnp.float32,
                )
            )
        taps.append(jnp.stack(line))
    return jnp.stack(taps)


def dsilu(value):
    sig = jax.nn.sigmoid(value)
    return sig * (1.0 + value * (1.0 - sig))


def shards(features, grad_out, kernel_one, kernel_two):
    slides, chans, rows, cols = features.shape
    feat_pad = extended(features, (("row", 2), ("col", 3)), 1)
    pre_one = convolve(feat_pad, kernel_one, rows, cols)
    hidden = jax.nn.silu(pre_one).astype(jnp.bfloat16)
    hid_pad = extended(hidden, (("row", 2), ("col", 3)), 1)
    pre_two = convolve(hid_pad, kernel_two, rows, cols)
    delta_two = (grad_out.astype(jnp.float32) * dsilu(pre_two)).astype(jnp.bfloat16)
    delta_two_pad = extended(delta_two, (("row", 2), ("col", 3)), 1)
    back_one = transposed(delta_two_pad, kernel_two, rows, cols)
    delta_one = (back_one * dsilu(pre_one)).astype(jnp.bfloat16)
    delta_one_pad = extended(delta_one, (("row", 2), ("col", 3)), 1)
    grad_features = transposed(delta_one_pad, kernel_one, rows, cols).astype(jnp.bfloat16)
    term_two = kernel_grad(hid_pad, delta_two, rows, cols)
    term_one = kernel_grad(feat_pad, delta_one, rows, cols)
    both = summed(jnp.stack([term_one, term_two])).reshape(2, *term_one.shape)
    summed_one, summed_two = both[0], both[1]
    count = slides * lax.axis_size("dp") * rows * lax.axis_size("row") * cols * lax.axis_size("col")
    scale = 1.0 / jnp.sqrt(jnp.float32(count))
    return (grad_features, summed_one * scale, summed_two * scale)


def solution(mesh):
    return jax.shard_map(
        shards,
        mesh=mesh,
        in_specs=(P("dp", None, "row", "col"), P("dp", None, "row", "col"), P(), P()),
        out_specs=(P("dp", None, "row", "col"), P(), P()),
        check_vma=False,
    )
```

```python
import functools

import jax
import jax.numpy as jnp
from jax import lax
from jax.experimental import pallas as pl
from jax.experimental.pallas import tpu as pltpu
from jax.sharding import PartitionSpec as P

MESH = pl.DeviceIdType.MESH
F32, BF16 = jnp.float32, jnp.bfloat16

C = 64
ROWS, COLS = 16, 256
REACH = 4
TALL = ROWS + 2 * REACH
WIDE = 3 * C
LANES = 128


def rounded(value):
    return value.astype(BF16).astype(F32)


def sigmoid(value):
    return 0.5 * jnp.tanh(0.5 * value) + 0.5


def dot(a, b):
    return jnp.dot(a, b, preferred_element_type=F32)


def fused_kernel(
    near_row, near_col,
    feat_ref, grad_ref, k1_ref, k2_ref,
    gf_ref, g1_ref, g2_ref,
    raw, taps, feat, grad, sides, side_in, weights, x3, h3, e3, d3, prod, slope,
    delta_two, delta_one, edges, gf_rows, gf_raw, total, packed,
    mine, landed, part, stacked, final, gathered,
    in_sem, out_sem, halo_send, halo_recv,
    scatter_send, scatter_recv, depth_send, depth_recv, gather_send, gather_recv,
):
    dp, row, col = lax.axis_index("dp"), lax.axis_index("row"), lax.axis_index("col")
    n_dp, n_row, n_col = lax.axis_size("dp"), lax.axis_size("row"), lax.axis_size("col")
    plane = n_dp * near_row * near_col
    far_rows = n_row // near_row
    depth = far_rows * (n_col // near_col)
    far_row, far_col = row // near_row, col // near_col
    me = (dp * near_row + row % near_row) * near_col + col % near_col
    layer = far_col * far_rows + far_row

    def in_plane(member):
        return (
            member // (near_row * near_col),
            far_row * near_row + member // near_col % near_row,
            far_col * near_col + member % near_col,
        )

    def in_depth(step):
        other = (layer + step) % depth
        return (
            dp,
            other % far_rows * near_row + row % near_row,
            other // far_rows * near_col + col % near_col,
        )

    up, down = (row + n_row - 1) % n_row, (row + 1) % n_row
    left, right = (col + n_col - 1) % n_col, (col + 1) % n_col

    loads = [
        pltpu.make_async_copy(src, dst, in_sem.at[i])
        for i, (src, dst) in enumerate(
            [(feat_ref, raw.at[0]), (grad_ref, raw.at[1]), (k1_ref, taps.at[0]), (k2_ref, taps.at[1])]
        )
    ]
    for load in loads:
        load.start()

    barrier = pltpu.get_barrier_semaphore()

    def greet(target):
        pl.semaphore_signal(barrier, inc=1, device_id=target, device_id_type=MESH)

    for target in [
        (dp, up, left), (dp, up, right), (dp, down, left), (dp, down, right),
        (dp, up, col), (dp, down, col), (dp, row, left), (dp, row, right),
    ]:
        greet(target)

    def greet_plane(step, carry):
        greet(in_plane((me + step) % plane))
        return carry

    def greet_depth(step, carry):
        greet(in_depth(step))
        return carry

    lax.fori_loop(1, plane, greet_plane, 0)
    lax.fori_loop(1, depth, greet_depth, 0)

    a = lax.broadcasted_iota(jnp.int32, (ROWS * 16, ROWS * 16), 0)
    b = lax.broadcasted_iota(jnp.int32, (ROWS * 16, ROWS * 16), 1)
    swap = jnp.where(a == b % 16 * 16 + b // 16, 1.0, 0.0).astype(BF16)

    for which, rows_ref, first in ((0, feat, REACH), (1, grad, 2)):
        loads[which].wait()
        for block in range(C // 16):
            cells = raw[which, pl.ds(block * 16, 16)].reshape(ROWS * 16, COLS)
            turned = dot(swap, cells).astype(BF16).reshape(ROWS, 16, COLS)
            rows_ref[pl.ds(first, ROWS), pl.ds(block * 16, 16), :] = turned

    lane = lax.broadcasted_iota(jnp.int32, (C, LANES), 1)

    for side in range(2):
        tile = jnp.zeros((C, LANES), F32)
        for rows_ref, first, turn in ((feat, REACH, 0), (grad, 2, 64)):
            for r in range(ROWS):
                at = ((r + 8) * 4 + turn) % LANES
                cells = rows_ref[first + r, :, pl.ds(side * LANES, LANES)].astype(F32)
                shift = at if side == 0 else (at + 4) % LANES
                if shift:
                    cells = pltpu.roll(cells, shift, 1)
                tile = jnp.where((lane >= at) & (lane < at + 4), cells, tile)
        sides[side] = tile.astype(BF16)

    pl.semaphore_wait(barrier, 8 + plane + depth - 2)

    def send(i, src, dst, target):
        return pltpu.make_async_remote_copy(
            src_ref=src, dst_ref=dst, send_sem=halo_send.at[i], recv_sem=halo_recv.at[i],
            device_id=target, device_id_type=MESH,
        )

    side_copies = [
        send(0, sides.at[1], side_in.at[0], (dp, row, right)),
        send(1, sides.at[0], side_in.at[1], (dp, row, left)),
        send(2, sides.at[1], side_in.at[2], (dp, down, right)),
        send(3, sides.at[1], side_in.at[3], (dp, up, right)),
        send(4, sides.at[0], side_in.at[4], (dp, down, left)),
        send(5, sides.at[0], side_in.at[5], (dp, up, left)),
        send(6, sides, side_in.at[pl.ds(6, 2)], (dp, down, col)),
        send(7, sides, side_in.at[pl.ds(8, 2)], (dp, up, col)),
    ]
    row_copies = [
        send(8, feat.at[pl.ds(REACH, REACH)], feat.at[pl.ds(REACH + ROWS, REACH)], (dp, up, col)),
        send(9, feat.at[pl.ds(ROWS, REACH)], feat.at[pl.ds(0, REACH)], (dp, down, col)),
        send(10, grad.at[pl.ds(2, 2)], grad.at[pl.ds(2 + ROWS, 2)], (dp, up, col)),
        send(11, grad.at[pl.ds(ROWS, 2)], grad.at[pl.ds(0, 2)], (dp, down, col)),
    ]
    for copy in side_copies + row_copies:
        copy.start()

    for i in range(2):
        loads[2 + i].wait()
        for ky in range(3):
            for kx in range(3):
                weights[i, pl.ds(ky * C, C), pl.ds(kx * C, C)] = taps[i, ky, kx]
                flipped = taps[i, 2 - ky, 2 - kx].astype(F32).T.astype(BF16)
                weights[3 - i, pl.ds(ky * C, C), pl.ds(kx * C, C)] = flipped
    delta_one[0] = jnp.zeros((C, COLS), BF16)
    delta_one[TALL - 5] = jnp.zeros((C, COLS), BF16)

    for copy in side_copies:
        copy.wait_recv()

    middle = (lane >= 32) & (lane < 96)

    def half_turn(value):
        return pltpu.roll(value, 64, 1)

    def joined(here, above, below):
        crossed = half_turn(jnp.where(lane < 64, below, above))
        return (
            jnp.where(middle, here, crossed),
            jnp.where(middle, half_turn(here), jnp.where(lane < 64, above, below)),
        )

    def arrived(i):
        return side_in[i].astype(F32)

    groups = [
        joined(arrived(0), arrived(2), arrived(3)),
        joined(sides[0].astype(F32), arrived(6), arrived(8)),
        joined(sides[1].astype(F32), arrived(7), arrived(9)),
        joined(arrived(1), arrived(4), arrived(5)),
    ]

    spot = lane // 4 - 8
    line = row * ROWS + spot
    on_map = (line >= 0) & (line < n_row * ROWS)
    shown = [
        jnp.where(on_map & ok, 1.0, 0.0)
        for ok in (col > 0, col >= 0, col >= 0, col < n_col - 1)
    ]
    column = lane % 4

    def side_conv(which, tiles):
        a, b, c, d = tiles
        west = [
            pltpu.roll(a, 1, 1), jnp.where(column == 0, pltpu.roll(a, 125, 1), pltpu.roll(b, 1, 1)),
            pltpu.roll(c, 1, 1), jnp.where(column == 0, pltpu.roll(c, 125, 1), pltpu.roll(d, 1, 1)),
        ]
        east = [
            jnp.where(column == 3, pltpu.roll(b, 3, 1), pltpu.roll(a, 127, 1)), pltpu.roll(b, 127, 1),
            jnp.where(column == 3, pltpu.roll(d, 3, 1), pltpu.roll(c, 127, 1)), pltpu.roll(d, 127, 1),
        ]
        stack = jnp.concatenate([jnp.concatenate(part, axis=1) for part in (west, list(tiles), east)], axis=0)
        out = dot(weights[which], stack.astype(BF16))
        return [
            pltpu.roll(out[0:C, at : at + LANES], 4, 1)
            + out[C : 2 * C, at : at + LANES]
            + pltpu.roll(out[2 * C : 3 * C, at : at + LANES], 124, 1)
            for at in range(0, 4 * LANES, LANES)
        ]

    def keep(which, tiles):
        edges[which, 0] = tiles[0]
        edges[which, 1] = tiles[3]

    feat_tiles = [tile * ok for (tile, _), ok in zip(groups, shown)]
    keep(0, feat_tiles)
    pre = side_conv(0, feat_tiles)
    gates = [sigmoid(v) for v in pre]
    tiles = [rounded(v * s) * ok for v, s, ok in zip(pre, gates, shown)]
    keep(1, tiles)
    slopes = [s * (1.0 + v * (1.0 - s)) for v, s in zip(pre, gates)]
    pre = side_conv(1, tiles)
    gates = [sigmoid(v) for v in pre]
    tiles = [rounded(g * (s * (1.0 + v * (1.0 - s)))) * ok for v, s, (_, g), ok in zip(pre, gates, groups, shown)]
    keep(2, tiles)
    back = side_conv(2, tiles)
    keep(3, [rounded(v * s) * ok for v, s, ok in zip(back, slopes, shown)])

    for copy in row_copies:
        copy.wait_recv()

    def valid(j):
        at = row * ROWS + j - REACH
        return jnp.where((at >= 0) & (at < n_row * ROWS), 1.0, 0.0).astype(F32)

    def owned(j):
        return jnp.where((j >= REACH) & (j < REACH + ROWS), 1.0, 0.0).astype(F32)

    def widened(value, which, j):
        base = (j + 4) * 4
        west = pltpu.roll(value, 1, 1)
        east = pltpu.roll(value, COLS - 1, 1)
        first = pltpu.roll(edges[which, 0], 125 - base, 1)
        last = pltpu.roll(edges[which, 1], 127 - base, 1)
        west = jnp.concatenate([jnp.where(lane == 0, first, west[:, :LANES]), west[:, LANES:]], axis=1)
        east = jnp.concatenate([east[:, :LANES], jnp.where(lane == LANES - 1, last, east[:, LANES:])], axis=1)
        return jnp.concatenate([west, value, east], axis=0).astype(BF16)

    def widen_features(step, carry):
        for u in range(2):
            j = step * 2 + u
            x3[j] = widened(feat[j].astype(F32) * valid(j), 0, j)
        return carry

    lax.fori_loop(0, TALL // 2, widen_features, 0)

    def conv(which, source, low, high, finish):
        matrix = weights[which]

        def multiply(step):
            for u in range(2):
                j = low + 2 * step + u
                prod[j] = dot(matrix, source[j])

        def complete(step):
            for u in range(2):
                j = low + 2 * step - 3 + u
                finish(j, prod[j - 1, 0:C] + prod[j, C : 2 * C] + prod[j + 1, 2 * C : 3 * C])

        def both(step, carry):
            complete(step)
            multiply(step)
            return carry

        steps = (high - low) // 2
        multiply(0)
        multiply(1)
        lax.fori_loop(2, steps, both, 0)
        complete(steps)

    def first_layer(j, value):
        gate = sigmoid(value)
        slope[j] = gate * (1.0 + value * (1.0 - gate))
        h3[j] = widened(rounded(value * gate) * valid(j), 1, j)

    def second_layer(j, value):
        gate = sigmoid(value)
        delta = rounded(grad[j - 2].astype(F32) * (gate * (1.0 + value * (1.0 - gate)))) * valid(j)
        delta_two[j - 2] = (delta * owned(j)).astype(BF16)
        e3[j] = widened(delta, 2, j)

    def second_back(j, value):
        delta = rounded(value * slope[j]) * valid(j)
        delta_one[j - 2] = (delta * owned(j)).astype(BF16)
        d3[j] = widened(delta, 3, j)

    def first_back(j, value):
        gf_rows[j - REACH] = value.astype(BF16)

    def kernel_grad(which, delta, source):
        total[:, 0:WIDE] = jnp.zeros((WIDE, WIDE), F32)

        def add(step, carry):
            parts = []
            for u in range(2):
                s = step * 2 + u
                parts.append(lax.dot_general(
                    delta[pl.ds(s, 3)].reshape(WIDE, COLS), source[s + 3],
                    (((1,), (1,)), ((), ())), preferred_element_type=F32))
            total[:, 0:WIDE] += parts[0] + parts[1]
            return carry

        lax.fori_loop(0, (ROWS + 2) // 2, add, 0)
        packed[which, 0:WIDE] = total[:, 0:LANES]
        half = WIDE // 2
        slim = lax.broadcasted_iota(jnp.int32, (half, LANES), 1)
        packed[which, WIDE : WIDE + half] = jnp.where(
            slim < C, total[0:half, LANES : 2 * LANES], pltpu.roll(total[half:WIDE, LANES : 2 * LANES], C, 1))
        chunk = mine.shape[2]
        for j in range(plane):
            mine[which, j] = packed[which, j * chunk : (j + 1) * chunk]

    def scatter(which):
        def start(step, carry):
            other = (me + step) % plane
            pltpu.make_async_remote_copy(
                src_ref=mine.at[which, other], dst_ref=landed.at[which, step - 1],
                send_sem=scatter_send.at[which], recv_sem=scatter_recv.at[which],
                device_id=in_plane(other), device_id_type=MESH).start()
            return carry

        lax.fori_loop(1, plane, start, 0)

    def exchange(which):
        pltpu.make_async_copy(landed.at[which], landed.at[which], scatter_recv.at[which]).wait()
        part[which] = mine[which, me] + jnp.sum(landed[which], axis=0)
        stacked[which, layer] = part[which]

        def start(step, carry):
            pltpu.make_async_remote_copy(
                src_ref=part.at[which], dst_ref=stacked.at[which, layer],
                send_sem=depth_send.at[which], recv_sem=depth_recv.at[which],
                device_id=in_depth(step), device_id_type=MESH).start()
            return carry

        lax.fori_loop(1, depth, start, 0)

    def others(which):
        return stacked.at[which, pl.ds(0, depth - 1)]

    def members(which):
        return gathered.at[which, pl.ds(0, plane - 1)]

    def spread(which):
        pltpu.make_async_copy(others(which), others(which), depth_recv.at[which]).wait()
        final[which] = jnp.sum(stacked[which], axis=0) * (1.0 / (n_dp * n_row * ROWS * n_col * COLS) ** 0.5)
        gathered[which, me] = final[which]

        def start(step, carry):
            pltpu.make_async_remote_copy(
                src_ref=final.at[which], dst_ref=gathered.at[which, me],
                send_sem=gather_send.at[which], recv_sem=gather_recv.at[which],
                device_id=in_plane((me + step) % plane), device_id_type=MESH).start()
            return carry

        lax.fori_loop(1, plane, start, 0)

    def collect(which, out_ref):
        pltpu.make_async_copy(members(which), members(which), gather_recv.at[which]).wait()
        chunk = mine.shape[2]
        for j in range(plane):
            packed[which, j * chunk : (j + 1) * chunk] = gathered[which, j]
        half = WIDE // 2
        for ky in range(3):
            at = (2 - ky) * C
            for kx in range(2):
                out_ref[ky, kx] = packed[which, at : at + C, kx * C : (kx + 1) * C]
            cut = min(max(half - at, 0), C)
            if cut:
                out_ref[ky, 2, 0:cut] = packed[which, WIDE + at : WIDE + at + cut, 0:C]
            if cut < C:
                start = WIDE + at + cut - half
                out_ref[ky, 2, cut:C] = packed[which, start : start + C - cut, C : 2 * C]

    conv(0, x3, 0, TALL, first_layer)
    conv(1, h3, 1, TALL - 1, second_layer)
    kernel_grad(0, delta_two, h3)
    scatter(0)
    conv(2, e3, 2, TALL - 2, second_back)
    kernel_grad(1, delta_one, x3)
    scatter(1)
    exchange(0)
    conv(3, d3, 3, TALL - 3, first_back)
    for block in range(C // 16):
        cells = gf_rows[:, pl.ds(block * 16, 16), :].reshape(ROWS * 16, COLS)
        gf_raw[pl.ds(block * 16, 16)] = dot(swap, cells).astype(BF16).reshape(16, ROWS, COLS)
    store = pltpu.make_async_copy(gf_raw, gf_ref, out_sem)
    store.start()
    exchange(1)
    spread(0)
    spread(1)
    collect(0, g2_ref)
    collect(1, g1_ref)
    store.wait()
    for copy in side_copies + row_copies:
        copy.wait_send()
    for which in range(2):
        pltpu.make_async_copy(landed.at[which], landed.at[which], scatter_send.at[which]).wait()
        pltpu.make_async_copy(others(which), others(which), depth_send.at[which]).wait()
        pltpu.make_async_copy(members(which), members(which), gather_send.at[which]).wait()


def shards(near_row, near_col, features, grad_out, kernel_one, kernel_two):
    plane = lax.axis_size("dp") * near_row * near_col
    depth = lax.axis_size("row") // near_row * (lax.axis_size("col") // near_col)
    chunk = 9 * C * C // LANES // plane
    anywhere = pl.BlockSpec(memory_space=pl.ANY)
    vmem = pl.BlockSpec(memory_space=pltpu.VMEM)
    dma = pltpu.SemaphoreType.DMA
    stack = pltpu.VMEM((TALL, WIDE, COLS), BF16)
    gf, g1, g2 = pl.pallas_call(
        functools.partial(fused_kernel, near_row, near_col),
        out_shape=(
            jax.ShapeDtypeStruct((C, ROWS, COLS), BF16),
            jax.ShapeDtypeStruct((3, 3, C, C), F32),
            jax.ShapeDtypeStruct((3, 3, C, C), F32),
        ),
        in_specs=[anywhere] * 4,
        out_specs=(anywhere, vmem, vmem),
        scratch_shapes=[
            pltpu.VMEM((2, C, ROWS, COLS), BF16),
            pltpu.VMEM((2, 3, 3, C, C), BF16),
            pltpu.VMEM((TALL, C, COLS), BF16),
            pltpu.VMEM((TALL - 4, C, COLS), BF16),
            pltpu.VMEM((2, C, LANES), BF16),
            pltpu.VMEM((10, C, LANES), BF16),
            pltpu.VMEM((4, WIDE, WIDE), BF16),
            stack, stack, stack, stack,
            pltpu.VMEM((TALL, WIDE, COLS), F32),
            pltpu.VMEM((TALL, C, COLS), F32),
            pltpu.VMEM((TALL - 4, C, COLS), BF16),
            pltpu.VMEM((TALL - 4, C, COLS), BF16),
            pltpu.VMEM((4, 2, C, LANES), F32),
            pltpu.VMEM((ROWS, C, COLS), BF16),
            pltpu.VMEM((C, ROWS, COLS), BF16),
            pltpu.VMEM((WIDE, COLS), F32),
            pltpu.VMEM((2, 9 * C * C // LANES, LANES), F32),
            pltpu.VMEM((2, plane, chunk, LANES), F32),
            pltpu.VMEM((2, plane - 1, chunk, LANES), F32),
            pltpu.VMEM((2, chunk, LANES), F32),
            pltpu.VMEM((2, depth, chunk, LANES), F32),
            pltpu.VMEM((2, chunk, LANES), F32),
            pltpu.VMEM((2, plane, chunk, LANES), F32),
            dma((4,)), dma, dma((12,)), dma((12,)),
            dma((2,)), dma((2,)), dma((2,)), dma((2,)), dma((2,)), dma((2,)),
        ],
        compiler_params=pltpu.CompilerParams(collective_id=0, has_side_effects=True),
    )(features.reshape(C, ROWS, COLS), grad_out.reshape(C, ROWS, COLS), kernel_one, kernel_two)
    return gf.reshape(features.shape), g1, g2


def solution(mesh, near_row=4, near_col=4):
    return jax.shard_map(
        functools.partial(shards, near_row, near_col),
        mesh=mesh,
        in_specs=(P("dp", None, "row", "col"), P("dp", None, "row", "col"), P(), P()),
        out_specs=(P("dp", None, "row", "col"), P(), P()),
        check_vma=False,
    )
```

```python
import functools

import jax
import jax.numpy as jnp
from jax import lax
from jax.experimental import pallas as pl
from jax.experimental.pallas import tpu as pltpu
from jax.sharding import PartitionSpec as P

MESH = pl.DeviceIdType.MESH
F32, BF16 = jnp.float32, jnp.bfloat16

C = 64
ROWS, COLS = 16, 256
REACH = 4
TALL = ROWS + 2 * REACH
WIDE = 3 * C
LANES = 128
GROUP = 4
SPAN = 6


def rounded(value):
    return value.astype(BF16).astype(F32)


def sigmoid(value):
    return 0.5 * jnp.tanh(0.5 * value) + 0.5


def dot(a, b):
    return jnp.dot(a, b, preferred_element_type=F32)


def fused_kernel(
    near_row, near_col,
    feat_ref, grad_ref, k1_ref, k2_ref,
    gf_ref, g1_ref, g2_ref,
    raw, taps, feat, grad, sides, side_in, weights, x3, h3, e3, d3, prod, slope,
    delta_two, delta_one, edges, gf_rows, gf_raw, total, packed,
    mine, landed, part, stacked, final, gathered,
    in_sem, out_sem, halo_send, halo_recv,
    scatter_send, scatter_recv, depth_send, depth_recv, gather_send, gather_recv,
):
    dp, row, col = lax.axis_index("dp"), lax.axis_index("row"), lax.axis_index("col")
    n_dp, n_row, n_col = lax.axis_size("dp"), lax.axis_size("row"), lax.axis_size("col")
    plane = n_dp * near_row * near_col
    far_rows = n_row // near_row
    depth = far_rows * (n_col // near_col)
    far_row, far_col = row // near_row, col // near_col
    me = (dp * near_row + row % near_row) * near_col + col % near_col
    layer = far_col * far_rows + far_row

    def in_plane(member):
        return (
            member // (near_row * near_col),
            far_row * near_row + member // near_col % near_row,
            far_col * near_col + member % near_col,
        )

    def in_depth(step):
        other = (layer + step) % depth
        return (
            dp,
            other % far_rows * near_row + row % near_row,
            other // far_rows * near_col + col % near_col,
        )

    up, down = (row + n_row - 1) % n_row, (row + 1) % n_row
    left, right = (col + n_col - 1) % n_col, (col + 1) % n_col

    loads = [
        pltpu.make_async_copy(src, dst, in_sem.at[i])
        for i, (src, dst) in enumerate(
            [(feat_ref, raw.at[0]), (grad_ref, raw.at[1]), (k1_ref, taps.at[0]), (k2_ref, taps.at[1])]
        )
    ]
    for load in loads:
        load.start()

    barrier = pltpu.get_barrier_semaphore()

    def greet(target):
        pl.semaphore_signal(barrier, inc=1, device_id=target, device_id_type=MESH)

    for target in [
        (dp, up, left), (dp, up, right), (dp, down, left), (dp, down, right),
        (dp, up, col), (dp, down, col), (dp, row, left), (dp, row, right),
    ]:
        greet(target)

    def greet_plane(step, carry):
        greet(in_plane((me + step) % plane))
        return carry

    def greet_depth(step, carry):
        greet(in_depth(step))
        return carry

    lax.fori_loop(1, plane, greet_plane, 0)
    lax.fori_loop(1, depth, greet_depth, 0)

    a = lax.broadcasted_iota(jnp.int32, (ROWS * 16, ROWS * 16), 0)
    b = lax.broadcasted_iota(jnp.int32, (ROWS * 16, ROWS * 16), 1)
    swap = jnp.where(a == b % 16 * 16 + b // 16, 1.0, 0.0).astype(BF16)

    for which, rows_ref, first in ((0, feat, REACH), (1, grad, 2)):
        loads[which].wait()
        for block in range(C // 16):
            cells = raw[which, pl.ds(block * 16, 16)].reshape(ROWS * 16, COLS)
            turned = dot(swap, cells).astype(BF16).reshape(ROWS, 16, COLS)
            rows_ref[pl.ds(first, ROWS), pl.ds(block * 16, 16), :] = turned

    lane = lax.broadcasted_iota(jnp.int32, (C, LANES), 1)

    for side in range(2):
        tile = jnp.zeros((C, LANES), F32)
        for rows_ref, first, turn in ((feat, REACH, 0), (grad, 2, 64)):
            for r in range(ROWS):
                at = ((r + 8) * 4 + turn) % LANES
                cells = rows_ref[first + r, :, pl.ds(side * LANES, LANES)].astype(F32)
                shift = at if side == 0 else (at + 4) % LANES
                if shift:
                    cells = pltpu.roll(cells, shift, 1)
                tile = jnp.where((lane >= at) & (lane < at + 4), cells, tile)
        sides[side] = tile.astype(BF16)

    pl.semaphore_wait(barrier, 8 + plane + depth - 2)

    def send(i, src, dst, target):
        return pltpu.make_async_remote_copy(
            src_ref=src, dst_ref=dst, send_sem=halo_send.at[i], recv_sem=halo_recv.at[i],
            device_id=target, device_id_type=MESH,
        )

    side_copies = [
        send(0, sides.at[1], side_in.at[0], (dp, row, right)),
        send(1, sides.at[0], side_in.at[1], (dp, row, left)),
        send(2, sides.at[1], side_in.at[2], (dp, down, right)),
        send(3, sides.at[1], side_in.at[3], (dp, up, right)),
        send(4, sides.at[0], side_in.at[4], (dp, down, left)),
        send(5, sides.at[0], side_in.at[5], (dp, up, left)),
        send(6, sides, side_in.at[pl.ds(6, 2)], (dp, down, col)),
        send(7, sides, side_in.at[pl.ds(8, 2)], (dp, up, col)),
    ]
    row_copies = [
        send(8, feat.at[pl.ds(REACH, REACH)], feat.at[pl.ds(REACH + ROWS, REACH)], (dp, up, col)),
        send(9, feat.at[pl.ds(ROWS, REACH)], feat.at[pl.ds(0, REACH)], (dp, down, col)),
        send(10, grad.at[pl.ds(2, 2)], grad.at[pl.ds(2 + ROWS, 2)], (dp, up, col)),
        send(11, grad.at[pl.ds(ROWS, 2)], grad.at[pl.ds(0, 2)], (dp, down, col)),
    ]
    for copy in side_copies + row_copies:
        copy.start()

    for i in range(2):
        loads[2 + i].wait()
        for ky in range(3):
            for kx in range(3):
                weights[i, pl.ds(ky * C, C), pl.ds(kx * C, C)] = taps[i, ky, kx]
                flipped = taps[i, 2 - ky, 2 - kx].astype(F32).T.astype(BF16)
                weights[3 - i, pl.ds(ky * C, C), pl.ds(kx * C, C)] = flipped
    for rows_ref in (delta_one, delta_two):
        for r in (0, 1, ROWS + 2, ROWS + 3):
            rows_ref[r] = jnp.zeros((C, COLS), BF16)

    for copy in side_copies:
        copy.wait_recv()

    middle = (lane >= 32) & (lane < 96)

    def half_turn(value):
        return pltpu.roll(value, 64, 1)

    def joined(here, above, below):
        crossed = half_turn(jnp.where(lane < 64, below, above))
        return (
            jnp.where(middle, here, crossed),
            jnp.where(middle, half_turn(here), jnp.where(lane < 64, above, below)),
        )

    def arrived(i):
        return side_in[i].astype(F32)

    groups = [
        joined(arrived(0), arrived(2), arrived(3)),
        joined(sides[0].astype(F32), arrived(6), arrived(8)),
        joined(sides[1].astype(F32), arrived(7), arrived(9)),
        joined(arrived(1), arrived(4), arrived(5)),
    ]

    spot = lane // 4 - 8
    line = row * ROWS + spot
    on_map = (line >= 0) & (line < n_row * ROWS)
    shown = [
        jnp.where(on_map & ok, 1.0, 0.0)
        for ok in (col > 0, col >= 0, col >= 0, col < n_col - 1)
    ]
    column = lane % 4

    def side_conv(which, tiles):
        a, b, c, d = tiles
        west = [
            pltpu.roll(a, 1, 1), jnp.where(column == 0, pltpu.roll(a, 125, 1), pltpu.roll(b, 1, 1)),
            pltpu.roll(c, 1, 1), jnp.where(column == 0, pltpu.roll(c, 125, 1), pltpu.roll(d, 1, 1)),
        ]
        east = [
            jnp.where(column == 3, pltpu.roll(b, 3, 1), pltpu.roll(a, 127, 1)), pltpu.roll(b, 127, 1),
            jnp.where(column == 3, pltpu.roll(d, 3, 1), pltpu.roll(c, 127, 1)), pltpu.roll(d, 127, 1),
        ]
        stack = jnp.concatenate([jnp.concatenate(part, axis=1) for part in (west, list(tiles), east)], axis=0)
        out = dot(weights[which], stack.astype(BF16))
        return [
            pltpu.roll(out[0:C, at : at + LANES], 4, 1)
            + out[C : 2 * C, at : at + LANES]
            + pltpu.roll(out[2 * C : 3 * C, at : at + LANES], 124, 1)
            for at in range(0, 4 * LANES, LANES)
        ]

    def keep(which, tiles):
        edges[which, 0] = tiles[0]
        edges[which, 1] = tiles[3]

    feat_tiles = [tile * ok for (tile, _), ok in zip(groups, shown)]
    keep(0, feat_tiles)
    pre = side_conv(0, feat_tiles)
    gates = [sigmoid(v) for v in pre]
    tiles = [rounded(v * s) * ok for v, s, ok in zip(pre, gates, shown)]
    keep(1, tiles)
    slopes = [s * (1.0 + v * (1.0 - s)) for v, s in zip(pre, gates)]
    pre = side_conv(1, tiles)
    gates = [sigmoid(v) for v in pre]
    tiles = [rounded(g * (s * (1.0 + v * (1.0 - s)))) * ok for v, s, (_, g), ok in zip(pre, gates, groups, shown)]
    keep(2, tiles)
    back = side_conv(2, tiles)
    keep(3, [rounded(v * s) * ok for v, s, ok in zip(back, slopes, shown)])

    def valid(j):
        at = row * ROWS + j - REACH
        return jnp.where((at >= 0) & (at < n_row * ROWS), 1.0, 0.0).astype(F32)

    def own(j):
        return REACH <= j < REACH + ROWS

    def masked(value, j):
        return value if own(j) else value * valid(j)

    def widened(value, which, j):
        base = (j + 4) * 4
        west = pltpu.roll(value, 1, 1)
        east = pltpu.roll(value, COLS - 1, 1)
        first = pltpu.roll(edges[which, 0], 125 - base, 1)
        last = pltpu.roll(edges[which, 1], 127 - base, 1)
        west = jnp.concatenate([jnp.where(lane == 0, first, west[:, :LANES]), west[:, LANES:]], axis=1)
        east = jnp.concatenate([east[:, :LANES], jnp.where(lane == LANES - 1, last, east[:, LANES:])], axis=1)
        return jnp.concatenate([west, value, east], axis=0).astype(BF16)

    def widen_features(group):
        for j in group:
            x3[j] = widened(masked(feat[j].astype(F32), j), 0, j)

    def conv(which, source, reach, finish, prepare=None, gate=None):
        matrix = weights[which]

        def multiply(group):
            for j in group:
                prod[j] = dot(matrix, source[j])

        def complete(group):
            for j in group:
                finish(j, prod[j - 1, 0:C] + prod[j, C : 2 * C] + prod[j + 1, 2 * C : 3 * C])

        first, last = REACH, REACH + ROWS
        groups = [range(at, at + GROUP) for at in range(first, last, GROUP)]
        ready = first + 1
        if prepare:
            prepare(groups[0])
        for i, group in enumerate(groups):
            if prepare and i + 1 < len(groups):
                prepare(groups[i + 1])
            if i:
                complete(range(ready, group[0] - 1))
                ready = max(ready, group[0] - 1)
            multiply(group)
        border = list(range(first - reach, first)) + list(range(last, last + reach))
        if gate:
            complete(range(ready, last - 1))
            gate()
            prepare(border)
            multiply(border)
        else:
            multiply(border)
            complete(range(ready, last - 1))
        complete(range(first - reach + 1, first + 1))
        complete(range(last - 1, last + reach - 1))

    def first_layer(j, value):
        gate = sigmoid(value)
        if TALL - 4 > j - 1 >= 2:
            slope[j] = gate * (1.0 + value * (1.0 - gate))
        h3[j] = widened(masked(rounded(value * gate), j), 1, j)

    def second_layer(j, value):
        gate = sigmoid(value)
        delta = masked(rounded(grad[j - 2].astype(F32) * (gate * (1.0 + value * (1.0 - gate)))), j)
        if own(j):
            delta_two[j - 2] = delta.astype(BF16)
        e3[j] = widened(delta, 2, j)

    def second_back(j, value):
        delta = masked(rounded(value * slope[j]), j)
        if own(j):
            delta_one[j - 2] = delta.astype(BF16)
        d3[j] = widened(delta, 3, j)

    def first_back(j, value):
        gf_rows[j - REACH] = value.astype(BF16)

    def rows_in():
        for copy in row_copies:
            copy.wait_recv()

    def kernel_grad(which, delta, source):
        for at in range(0, ROWS + 2, SPAN):
            steps = range(at, at + SPAN)
            piece = lax.dot_general(
                jnp.concatenate([delta[s : s + 3].reshape(WIDE, COLS) for s in steps], axis=1),
                jnp.concatenate([source[s + 3] for s in steps], axis=1),
                (((1,), (1,)), ((), ())), preferred_element_type=F32)
            total[:, 0:WIDE] = piece if at == 0 else total[:, 0:WIDE] + piece
        packed[which, 0:WIDE] = total[:, 0:LANES]
        half = WIDE // 2
        slim = lax.broadcasted_iota(jnp.int32, (half, LANES), 1)
        packed[which, WIDE : WIDE + half] = jnp.where(
            slim < C, total[0:half, LANES : 2 * LANES], pltpu.roll(total[half:WIDE, LANES : 2 * LANES], C, 1))
        chunk = mine.shape[2]
        for j in range(plane):
            mine[which, j] = packed[which, j * chunk : (j + 1) * chunk]

    def scatter(which):
        def start(step, carry):
            other = (me + step) % plane
            pltpu.make_async_remote_copy(
                src_ref=mine.at[which, other], dst_ref=landed.at[which, step - 1],
                send_sem=scatter_send.at[which], recv_sem=scatter_recv.at[which],
                device_id=in_plane(other), device_id_type=MESH).start()
            return carry

        lax.fori_loop(1, plane, start, 0)

    def exchange(which):
        pltpu.make_async_copy(landed.at[which], landed.at[which], scatter_recv.at[which]).wait()
        part[which] = mine[which, me] + jnp.sum(landed[which], axis=0)
        stacked[which, layer] = part[which]

        def start(step, carry):
            pltpu.make_async_remote_copy(
                src_ref=part.at[which], dst_ref=stacked.at[which, layer],
                send_sem=depth_send.at[which], recv_sem=depth_recv.at[which],
                device_id=in_depth(step), device_id_type=MESH).start()
            return carry

        lax.fori_loop(1, depth, start, 0)

    def others(which):
        return stacked.at[which, pl.ds(0, depth - 1)]

    def members(which):
        return gathered.at[which, pl.ds(0, plane - 1)]

    def spread(which):
        pltpu.make_async_copy(others(which), others(which), depth_recv.at[which]).wait()
        final[which] = jnp.sum(stacked[which], axis=0) * (1.0 / (n_dp * n_row * ROWS * n_col * COLS) ** 0.5)
        gathered[which, me] = final[which]

        def start(step, carry):
            pltpu.make_async_remote_copy(
                src_ref=final.at[which], dst_ref=gathered.at[which, me],
                send_sem=gather_send.at[which], recv_sem=gather_recv.at[which],
                device_id=in_plane((me + step) % plane), device_id_type=MESH).start()
            return carry

        lax.fori_loop(1, plane, start, 0)

    def collect(which, out_ref):
        pltpu.make_async_copy(members(which), members(which), gather_recv.at[which]).wait()
        chunk = mine.shape[2]
        for j in range(plane):
            packed[which, j * chunk : (j + 1) * chunk] = gathered[which, j]
        half = WIDE // 2
        for ky in range(3):
            at = (2 - ky) * C
            for kx in range(2):
                out_ref[ky, kx] = packed[which, at : at + C, kx * C : (kx + 1) * C]
            cut = min(max(half - at, 0), C)
            if cut:
                out_ref[ky, 2, 0:cut] = packed[which, WIDE + at : WIDE + at + cut, 0:C]
            if cut < C:
                start = WIDE + at + cut - half
                out_ref[ky, 2, cut:C] = packed[which, start : start + C - cut, C : 2 * C]

    conv(0, x3, 4, first_layer, widen_features, rows_in)
    conv(1, h3, 3, second_layer)
    kernel_grad(0, delta_two, h3)
    scatter(0)
    conv(2, e3, 2, second_back)
    kernel_grad(1, delta_one, x3)
    scatter(1)
    exchange(0)
    conv(3, d3, 1, first_back)
    for block in range(C // 16):
        cells = gf_rows[:, pl.ds(block * 16, 16), :].reshape(ROWS * 16, COLS)
        gf_raw[pl.ds(block * 16, 16)] = dot(swap, cells).astype(BF16).reshape(16, ROWS, COLS)
    store = pltpu.make_async_copy(gf_raw, gf_ref, out_sem)
    store.start()
    exchange(1)
    spread(0)
    spread(1)
    collect(0, g2_ref)
    collect(1, g1_ref)
    store.wait()
    for copy in side_copies + row_copies:
        copy.wait_send()
    for which in range(2):
        pltpu.make_async_copy(landed.at[which], landed.at[which], scatter_send.at[which]).wait()
        pltpu.make_async_copy(others(which), others(which), depth_send.at[which]).wait()
        pltpu.make_async_copy(members(which), members(which), gather_send.at[which]).wait()


def shards(near_row, near_col, features, grad_out, kernel_one, kernel_two):
    plane = lax.axis_size("dp") * near_row * near_col
    depth = lax.axis_size("row") // near_row * (lax.axis_size("col") // near_col)
    chunk = 9 * C * C // LANES // plane
    anywhere = pl.BlockSpec(memory_space=pl.ANY)
    vmem = pl.BlockSpec(memory_space=pltpu.VMEM)
    dma = pltpu.SemaphoreType.DMA
    stack = pltpu.VMEM((TALL, WIDE, COLS), BF16)
    gf, g1, g2 = pl.pallas_call(
        functools.partial(fused_kernel, near_row, near_col),
        out_shape=(
            jax.ShapeDtypeStruct((C, ROWS, COLS), BF16),
            jax.ShapeDtypeStruct((3, 3, C, C), F32),
            jax.ShapeDtypeStruct((3, 3, C, C), F32),
        ),
        in_specs=[anywhere] * 4,
        out_specs=(anywhere, vmem, vmem),
        scratch_shapes=[
            pltpu.VMEM((2, C, ROWS, COLS), BF16),
            pltpu.VMEM((2, 3, 3, C, C), BF16),
            pltpu.VMEM((TALL, C, COLS), BF16),
            pltpu.VMEM((TALL - 4, C, COLS), BF16),
            pltpu.VMEM((2, C, LANES), BF16),
            pltpu.VMEM((10, C, LANES), BF16),
            pltpu.VMEM((4, WIDE, WIDE), BF16),
            stack, stack, stack, stack,
            pltpu.VMEM((TALL, WIDE, COLS), F32),
            pltpu.VMEM((TALL, C, COLS), F32),
            pltpu.VMEM((TALL - 4, C, COLS), BF16),
            pltpu.VMEM((TALL - 4, C, COLS), BF16),
            pltpu.VMEM((4, 2, C, LANES), F32),
            pltpu.VMEM((ROWS, C, COLS), BF16),
            pltpu.VMEM((C, ROWS, COLS), BF16),
            pltpu.VMEM((WIDE, COLS), F32),
            pltpu.VMEM((2, 9 * C * C // LANES, LANES), F32),
            pltpu.VMEM((2, plane, chunk, LANES), F32),
            pltpu.VMEM((2, plane - 1, chunk, LANES), F32),
            pltpu.VMEM((2, chunk, LANES), F32),
            pltpu.VMEM((2, depth, chunk, LANES), F32),
            pltpu.VMEM((2, chunk, LANES), F32),
            pltpu.VMEM((2, plane, chunk, LANES), F32),
            dma((4,)), dma, dma((12,)), dma((12,)),
            dma((2,)), dma((2,)), dma((2,)), dma((2,)), dma((2,)), dma((2,)),
        ],
        compiler_params=pltpu.CompilerParams(collective_id=0, has_side_effects=True),
    )(features.reshape(C, ROWS, COLS), grad_out.reshape(C, ROWS, COLS), kernel_one, kernel_two)
    return gf.reshape(features.shape), g1, g2


def solution(mesh, near_row=4, near_col=4):
    return jax.shard_map(
        functools.partial(shards, near_row, near_col),
        mesh=mesh,
        in_specs=(P("dp", None, "row", "col"), P("dp", None, "row", "col"), P(), P()),
        out_specs=(P("dp", None, "row", "col"), P(), P()),
        check_vma=False,
    )
```

```python
import functools

import jax
import jax.numpy as jnp
from jax import lax
from jax.experimental import pallas as pl
from jax.experimental.pallas import tpu as pltpu
from jax.sharding import PartitionSpec as P

MESH = pl.DeviceIdType.MESH
F32, BF16 = jnp.float32, jnp.bfloat16

C = 64
ROWS, COLS = 16, 256
REACH = 4
TALL = ROWS + 2 * REACH
WIDE = 3 * C
LANES = 128
GROUP = 4
SPAN = 6
NEARER = ((0, 2), (1, 1), (1, 3), (0, 1), (0, 3), (1, 0), (3, 0), (0, 0))


def rounded(value):
    return value.astype(BF16).astype(F32)


def sigmoid(value):
    return 0.5 * jnp.tanh(0.5 * value) + 0.5


def dot(a, b):
    return jnp.dot(a, b, preferred_element_type=F32)


def fused_kernel(
    near_row, near_col,
    feat_ref, grad_ref, k1_ref, k2_ref,
    gf_ref, sums_ref,
    raw, taps, feat, grad, sides, side_in, weights, x3, h3, e3, d3, prod, slope,
    delta_two, delta_one, edges, gf_rows, gf_raw, total, packed,
    mine, landed, part, stacked, final, gathered,
    in_sem, out_sem, sum_sem, halo_send, halo_recv,
    scatter_send, scatter_recv, depth_send, depth_recv, gather_send, gather_recv,
):
    dp, row, col = lax.axis_index("dp"), lax.axis_index("row"), lax.axis_index("col")
    n_dp, n_row, n_col = lax.axis_size("dp"), lax.axis_size("row"), lax.axis_size("col")
    plane = n_dp * near_row * near_col
    far_rows = n_row // near_row
    depth = far_rows * (n_col // near_col)
    far_row, far_col = row // near_row, col // near_col
    me = (dp * near_row + row % near_row) * near_col + col % near_col
    layer = far_col * far_rows + far_row

    def in_depth(step):
        other = (layer + step) % depth
        return (
            dp,
            other % far_rows * near_row + row % near_row,
            other // far_rows * near_col + col % near_col,
        )

    def hops(step, size):
        return min(step, size - step)

    cores = [(dp + i) % n_dp for i in range(n_dp)]
    near_rows = [(row % near_row + i) % near_row for i in range(near_row)]
    near_cols = [(col % near_col + i) % near_col for i in range(near_col)]
    offsets = [(i, j, k) for i in range(n_dp) for j in range(near_row) for k in range(near_col)][1:]
    offsets.sort(key=lambda at: -hops(at[1], near_row) - hops(at[2], near_col))
    def chunk_of(core, y, x):
        return (core * (near_row // 2) + y % (near_row // 2)) * near_col + (x + y // (near_row // 2) * (near_col // 2)) % near_col

    def peer(at):
        i, j, k = at
        return (
            chunk_of(cores[i], near_rows[j], near_cols[k]),
            (cores[i], far_row * near_row + near_rows[j], far_col * near_col + near_cols[k]),
        )

    peers = [peer(at) for at in offsets]
    closer = [peer((i, j, k)) for i in range(n_dp) for j, k in NEARER if (i, j, k) != (0, 0, 0)]
    own_chunk = chunk_of(dp, row % near_row, col % near_col)
    above = [in_depth(step) for step in sorted(range(1, depth), key=lambda step: -hops(step, depth))]

    up, down = (row + n_row - 1) % n_row, (row + 1) % n_row
    left, right = (col + n_col - 1) % n_col, (col + 1) % n_col

    loads = [
        pltpu.make_async_copy(src, dst, in_sem.at[i])
        for i, (src, dst) in enumerate(
            [(feat_ref, raw.at[0]), (grad_ref, raw.at[1]), (k1_ref, taps.at[0]), (k2_ref, taps.at[1])]
        )
    ]
    for load in loads:
        load.start()

    barrier = pltpu.get_barrier_semaphore()

    def greet(target):
        pl.semaphore_signal(barrier, inc=1, device_id=target, device_id_type=MESH)

    for target in [
        (dp, up, left), (dp, up, right), (dp, down, left), (dp, down, right),
        (dp, up, col), (dp, down, col), (dp, row, left), (dp, row, right),
    ]:
        greet(target)

    for _, target in peers:
        greet(target)
    for target in above:
        greet(target)

    a = lax.broadcasted_iota(jnp.int32, (ROWS * 16, ROWS * 16), 0)
    b = lax.broadcasted_iota(jnp.int32, (ROWS * 16, ROWS * 16), 1)
    swap = jnp.where(a == b % 16 * 16 + b // 16, 1.0, 0.0).astype(BF16)

    for which, rows_ref, first in ((0, feat, REACH), (1, grad, 2)):
        loads[which].wait()
        for block in range(C // 16):
            cells = raw[which, pl.ds(block * 16, 16)].reshape(ROWS * 16, COLS)
            turned = dot(swap, cells).astype(BF16).reshape(ROWS, 16, COLS)
            rows_ref[pl.ds(first, ROWS), pl.ds(block * 16, 16), :] = turned

    lane = lax.broadcasted_iota(jnp.int32, (C, LANES), 1)

    for side in range(2):
        tile = jnp.zeros((C, LANES), F32)
        for rows_ref, first, turn in ((feat, REACH, 0), (grad, 2, 64)):
            for r in range(ROWS):
                at = ((r + 8) * 4 + turn) % LANES
                cells = rows_ref[first + r, :, pl.ds(side * LANES, LANES)].astype(F32)
                shift = at if side == 0 else (at + 4) % LANES
                if shift:
                    cells = pltpu.roll(cells, shift, 1)
                tile = jnp.where((lane >= at) & (lane < at + 4), cells, tile)
        sides[side] = tile.astype(BF16)

    pl.semaphore_wait(barrier, 8 + plane + depth - 2)

    def send(i, src, dst, target):
        return pltpu.make_async_remote_copy(
            src_ref=src, dst_ref=dst, send_sem=halo_send.at[i], recv_sem=halo_recv.at[i],
            device_id=target, device_id_type=MESH,
        )

    side_copies = [
        send(0, sides.at[1], side_in.at[0], (dp, row, right)),
        send(1, sides.at[0], side_in.at[1], (dp, row, left)),
        send(2, sides.at[1], side_in.at[2], (dp, down, right)),
        send(3, sides.at[1], side_in.at[3], (dp, up, right)),
        send(4, sides.at[0], side_in.at[4], (dp, down, left)),
        send(5, sides.at[0], side_in.at[5], (dp, up, left)),
        send(6, sides, side_in.at[pl.ds(6, 2)], (dp, down, col)),
        send(7, sides, side_in.at[pl.ds(8, 2)], (dp, up, col)),
    ]
    row_copies = [
        send(8, feat.at[pl.ds(REACH, REACH)], feat.at[pl.ds(REACH + ROWS, REACH)], (dp, up, col)),
        send(9, feat.at[pl.ds(ROWS, REACH)], feat.at[pl.ds(0, REACH)], (dp, down, col)),
        send(10, grad.at[pl.ds(2, 2)], grad.at[pl.ds(2 + ROWS, 2)], (dp, up, col)),
        send(11, grad.at[pl.ds(ROWS, 2)], grad.at[pl.ds(0, 2)], (dp, down, col)),
    ]
    for copy in side_copies + row_copies:
        copy.start()

    for i in range(2):
        loads[2 + i].wait()
        for ky in range(3):
            for kx in range(3):
                weights[i, pl.ds(ky * C, C), pl.ds(kx * C, C)] = taps[i, ky, kx]
                flipped = taps[i, 2 - ky, 2 - kx].astype(F32).T.astype(BF16)
                weights[3 - i, pl.ds(ky * C, C), pl.ds(kx * C, C)] = flipped
    for rows_ref in (delta_one, delta_two):
        for r in (0, 1, ROWS + 2, ROWS + 3):
            rows_ref[r] = jnp.zeros((C, COLS), BF16)

    for copy in side_copies:
        copy.wait_recv()

    middle = (lane >= 32) & (lane < 96)

    def half_turn(value):
        return pltpu.roll(value, 64, 1)

    def joined(here, above, below):
        crossed = half_turn(jnp.where(lane < 64, below, above))
        return (
            jnp.where(middle, here, crossed),
            jnp.where(middle, half_turn(here), jnp.where(lane < 64, above, below)),
        )

    def arrived(i):
        return side_in[i].astype(F32)

    groups = [
        joined(arrived(0), arrived(2), arrived(3)),
        joined(sides[0].astype(F32), arrived(6), arrived(8)),
        joined(sides[1].astype(F32), arrived(7), arrived(9)),
        joined(arrived(1), arrived(4), arrived(5)),
    ]

    spot = lane // 4 - 8
    line = row * ROWS + spot
    on_map = (line >= 0) & (line < n_row * ROWS)
    shown = [
        jnp.where(on_map & ok, 1.0, 0.0)
        for ok in (col > 0, col >= 0, col >= 0, col < n_col - 1)
    ]
    column = lane % 4

    def side_conv(which, tiles):
        a, b, c, d = tiles
        west = [
            pltpu.roll(a, 1, 1), jnp.where(column == 0, pltpu.roll(a, 125, 1), pltpu.roll(b, 1, 1)),
            pltpu.roll(c, 1, 1), jnp.where(column == 0, pltpu.roll(c, 125, 1), pltpu.roll(d, 1, 1)),
        ]
        east = [
            jnp.where(column == 3, pltpu.roll(b, 3, 1), pltpu.roll(a, 127, 1)), pltpu.roll(b, 127, 1),
            jnp.where(column == 3, pltpu.roll(d, 3, 1), pltpu.roll(c, 127, 1)), pltpu.roll(d, 127, 1),
        ]
        stack = jnp.concatenate([jnp.concatenate(part, axis=1) for part in (west, list(tiles), east)], axis=0)
        out = dot(weights[which], stack.astype(BF16))
        return [
            pltpu.roll(out[0:C, at : at + LANES], 4, 1)
            + out[C : 2 * C, at : at + LANES]
            + pltpu.roll(out[2 * C : 3 * C, at : at + LANES], 124, 1)
            for at in range(0, 4 * LANES, LANES)
        ]

    def keep(which, tiles):
        edges[which, 0] = tiles[0]
        edges[which, 1] = tiles[3]

    feat_tiles = [tile * ok for (tile, _), ok in zip(groups, shown)]
    keep(0, feat_tiles)
    pre = side_conv(0, feat_tiles)
    gates = [sigmoid(v) for v in pre]
    hidden_tiles = [rounded(v * s) * ok for v, s, ok in zip(pre, gates, shown)]
    keep(1, hidden_tiles)
    slopes = [s * (1.0 + v * (1.0 - s)) for v, s in zip(pre, gates)]
    def side_rest():
        pre = side_conv(1, hidden_tiles)
        gates = [sigmoid(v) for v in pre]
        tiles = [rounded(g * (s * (1.0 + v * (1.0 - s)))) * ok for v, s, (_, g), ok in zip(pre, gates, groups, shown)]
        keep(2, tiles)
        back = side_conv(2, tiles)
        keep(3, [rounded(v * s) * ok for v, s, ok in zip(back, slopes, shown)])

    def valid(j):
        at = row * ROWS + j - REACH
        return jnp.where((at >= 0) & (at < n_row * ROWS), 1.0, 0.0).astype(F32)

    def own(j):
        return REACH <= j < REACH + ROWS

    def masked(value, j):
        return value if own(j) else value * valid(j)

    def widened(value, which, j):
        base = (j + 4) * 4
        west = pltpu.roll(value, 1, 1)
        east = pltpu.roll(value, COLS - 1, 1)
        first = pltpu.roll(edges[which, 0], 125 - base, 1)
        last = pltpu.roll(edges[which, 1], 127 - base, 1)
        west = jnp.concatenate([jnp.where(lane == 0, first, west[:, :LANES]), west[:, LANES:]], axis=1)
        east = jnp.concatenate([east[:, :LANES], jnp.where(lane == LANES - 1, last, east[:, LANES:])], axis=1)
        return jnp.concatenate([west, value, east], axis=0).astype(BF16)

    def widen_features(group):
        for j in group:
            x3[j] = widened(masked(feat[j].astype(F32), j), 0, j)

    def conv(which, source, reach, finish, prepare=None, gate=None):
        matrix = weights[which]

        def multiply(group):
            for j in group:
                prod[j] = dot(matrix, source[j])

        def complete(group):
            for j in group:
                finish(j, prod[j - 1, 0:C] + prod[j, C : 2 * C] + prod[j + 1, 2 * C : 3 * C])

        first, last = REACH, REACH + ROWS
        groups = [range(at, at + GROUP) for at in range(first, last, GROUP)]
        ready = first + 1
        if prepare:
            prepare(groups[0])
        for i, group in enumerate(groups):
            if prepare and i + 1 < len(groups):
                prepare(groups[i + 1])
            if i:
                complete(range(ready, group[0] - 1))
                ready = max(ready, group[0] - 1)
            multiply(group)
        border = list(range(first - reach, first)) + list(range(last, last + reach))
        if gate:
            complete(range(ready, last - 1))
            gate()
            prepare(border)
            multiply(border)
        else:
            multiply(border)
            complete(range(ready, last - 1))
        complete(range(first - reach + 1, first + 1))
        complete(range(last - 1, last + reach - 1))

    def first_layer(j, value):
        gate = sigmoid(value)
        if TALL - 4 > j - 1 >= 2:
            slope[j] = gate * (1.0 + value * (1.0 - gate))
        h3[j] = widened(masked(rounded(value * gate), j), 1, j)

    def second_layer(j, value):
        gate = sigmoid(value)
        delta = masked(rounded(grad[j - 2].astype(F32) * (gate * (1.0 + value * (1.0 - gate)))), j)
        if own(j):
            delta_two[j - 2] = delta.astype(BF16)
        e3[j] = widened(delta, 2, j)

    def second_back(j, value):
        delta = masked(rounded(value * slope[j]), j)
        if own(j):
            delta_one[j - 2] = delta.astype(BF16)
        d3[j] = widened(delta, 3, j)

    def first_back(j, value):
        gf_rows[j - REACH] = value.astype(BF16)

    def rows_in():
        for copy in row_copies:
            copy.wait_recv()
        side_rest()

    def kernel_grad(which, delta, source):
        for at in range(0, ROWS + 2, SPAN):
            steps = range(at, at + SPAN)
            piece = lax.dot_general(
                jnp.concatenate([delta[s : s + 3].reshape(WIDE, COLS) for s in steps], axis=1),
                jnp.concatenate([source[s + 3] for s in steps], axis=1),
                (((1,), (1,)), ((), ())), preferred_element_type=F32)
            total[:, 0:WIDE] = piece if at == 0 else total[:, 0:WIDE] + piece
        packed[which, 0:WIDE] = total[:, 0:LANES]
        half = WIDE // 2
        slim = lax.broadcasted_iota(jnp.int32, (half, LANES), 1)
        packed[which, WIDE : WIDE + half] = jnp.where(
            slim < C, total[0:half, LANES : 2 * LANES], pltpu.roll(total[half:WIDE, LANES : 2 * LANES], C, 1))
        chunk = mine.shape[2]
        for j in range(plane // 2):
            mine[which, j] = packed[which, j * chunk : (j + 1) * chunk]

    def scatter(which):
        landed[which, me] = mine[which, own_chunk]
        for other, target in peers:
            pltpu.make_async_remote_copy(
                src_ref=mine.at[which, other], dst_ref=landed.at[which, me],
                send_sem=scatter_send.at[which], recv_sem=scatter_recv.at[which],
                device_id=target, device_id_type=MESH).start()

    def arrivals(which):
        return landed.at[which, pl.ds(0, plane - 1)]

    def exchange(which):
        pltpu.make_async_copy(arrivals(which), arrivals(which), scatter_recv.at[which]).wait()
        part[which] = jnp.sum(landed[which], axis=0)
        stacked[which, layer] = part[which]

        for target in above:
            pltpu.make_async_remote_copy(
                src_ref=part.at[which], dst_ref=stacked.at[which, layer],
                send_sem=depth_send.at[which], recv_sem=depth_recv.at[which],
                device_id=target, device_id_type=MESH).start()

    def others(which):
        return stacked.at[which, pl.ds(0, depth - 1)]

    def members(which):
        return gathered.at[which, pl.ds(0, plane // 2 - 1)]

    def spread(which):
        if depth > 1:
            pltpu.make_async_copy(others(which), others(which), depth_recv.at[which]).wait()
        final[which] = jnp.sum(stacked[which], axis=0) * (1.0 / (n_dp * n_row * ROWS * n_col * COLS) ** 0.5)
        gathered[which, own_chunk] = final[which]

        for _, target in closer:
            pltpu.make_async_remote_copy(
                src_ref=final.at[which], dst_ref=gathered.at[which, own_chunk],
                send_sem=gather_send.at[which], recv_sem=gather_recv.at[which],
                device_id=target, device_id_type=MESH).start()

    def collect(which):
        pltpu.make_async_copy(members(which), members(which), gather_recv.at[which]).wait()
        return pltpu.make_async_copy(gathered.at[which], sums_ref.at[which], sum_sem.at[which])

    conv(0, x3, 4, first_layer, widen_features, rows_in)
    conv(1, h3, 3, second_layer)
    kernel_grad(0, delta_two, h3)
    scatter(0)
    conv(2, e3, 2, second_back)
    kernel_grad(1, delta_one, x3)
    scatter(1)
    exchange(0)
    conv(3, d3, 1, first_back)
    for block in range(C // 16):
        cells = gf_rows[:, pl.ds(block * 16, 16), :].reshape(ROWS * 16, COLS)
        gf_raw[pl.ds(block * 16, 16)] = dot(swap, cells).astype(BF16).reshape(16, ROWS, COLS)
    store = pltpu.make_async_copy(gf_raw, gf_ref, out_sem)
    store.start()
    exchange(1)
    spread(0)
    spread(1)
    stores = [store, collect(0)]
    stores[1].start()
    stores.append(collect(1))
    stores[2].start()
    for store in stores:
        store.wait()
    for copy in side_copies + row_copies:
        copy.wait_send()
    for which in range(2):
        pltpu.make_async_copy(arrivals(which), arrivals(which), scatter_send.at[which]).wait()
        if depth > 1:
            pltpu.make_async_copy(others(which), others(which), depth_send.at[which]).wait()
        pltpu.make_async_copy(members(which), members(which), gather_send.at[which]).wait()


def output_kernel(gf_ref, sums_ref, out_ref, g1_ref, g2_ref, cells, sums, packed, taps, in_sem, out_sem):
    blocks = [pl.ds(at, C // 4) for at in range(0, C, C // 4)]
    sum_load = pltpu.make_async_copy(sums_ref, sums, in_sem.at[4])
    sum_load.start()
    loads = [pltpu.make_async_copy(gf_ref.at[at], cells.at[at], in_sem.at[i]) for i, at in enumerate(blocks)]
    stores = [pltpu.make_async_copy(cells.at[at], out_ref.at[at], out_sem.at[i]) for i, at in enumerate(blocks)]
    for load in loads:
        load.start()
    sum_load.wait()
    chunk = sums.shape[2]
    half = WIDE // 2
    for which, target in ((0, g2_ref), (1, g1_ref)):
        for j in range(sums.shape[1]):
            packed[which, j * chunk : (j + 1) * chunk] = sums[which, j]
        for ky in range(3):
            at = (2 - ky) * C
            for kx in range(2):
                taps[which, ky, kx] = packed[which, at : at + C, kx * C : (kx + 1) * C]
            cut = min(max(half - at, 0), C)
            if cut:
                taps[which, ky, 2, 0:cut] = packed[which, WIDE + at : WIDE + at + cut, 0:C]
            if cut < C:
                start = WIDE + at + cut - half
                taps[which, ky, 2, cut:C] = packed[which, start : start + C - cut, C : 2 * C]
        store = pltpu.make_async_copy(taps.at[which], target, out_sem.at[4 + which])
        store.start()
        stores.append(store)
    for load, store in zip(loads, stores):
        load.wait()
        store.start()
    for store in stores:
        store.wait()


def shards(near_row, near_col, features, grad_out, kernel_one, kernel_two):
    plane = lax.axis_size("dp") * near_row * near_col
    depth = lax.axis_size("row") // near_row * (lax.axis_size("col") // near_col)
    chunk = 9 * C * C // LANES // (plane // 2)
    anywhere = pl.BlockSpec(memory_space=pl.ANY)
    dma = pltpu.SemaphoreType.DMA
    stack = pltpu.VMEM((TALL, WIDE, COLS), BF16)
    gf, sums = pl.pallas_call(
        functools.partial(fused_kernel, near_row, near_col),
        out_shape=(
            jax.ShapeDtypeStruct((C, ROWS, COLS), BF16),
            jax.ShapeDtypeStruct((2, plane // 2, chunk, LANES), F32),
        ),
        in_specs=[anywhere] * 4,
        out_specs=(anywhere, anywhere),
        scratch_shapes=[
            pltpu.VMEM((2, C, ROWS, COLS), BF16),
            pltpu.VMEM((2, 3, 3, C, C), BF16),
            pltpu.VMEM((TALL, C, COLS), BF16),
            pltpu.VMEM((TALL - 4, C, COLS), BF16),
            pltpu.VMEM((2, C, LANES), BF16),
            pltpu.VMEM((10, C, LANES), BF16),
            pltpu.VMEM((4, WIDE, WIDE), BF16),
            stack, stack, stack, stack,
            pltpu.VMEM((TALL, WIDE, COLS), F32),
            pltpu.VMEM((TALL, C, COLS), F32),
            pltpu.VMEM((TALL - 4, C, COLS), BF16),
            pltpu.VMEM((TALL - 4, C, COLS), BF16),
            pltpu.VMEM((4, 2, C, LANES), F32),
            pltpu.VMEM((ROWS, C, COLS), BF16),
            pltpu.VMEM((C, ROWS, COLS), BF16),
            pltpu.VMEM((WIDE, COLS), F32),
            pltpu.VMEM((2, 9 * C * C // LANES, LANES), F32),
            pltpu.VMEM((2, plane // 2, chunk, LANES), F32),
            pltpu.VMEM((2, plane, chunk, LANES), F32),
            pltpu.VMEM((2, chunk, LANES), F32),
            pltpu.VMEM((2, depth, chunk, LANES), F32),
            pltpu.VMEM((2, chunk, LANES), F32),
            pltpu.VMEM((2, plane // 2, chunk, LANES), F32),
            dma((4,)), dma, dma((2,)), dma((12,)), dma((12,)),
            dma((2,)), dma((2,)), dma((2,)), dma((2,)), dma((2,)), dma((2,)),
        ],
        compiler_params=pltpu.CompilerParams(collective_id=0, has_side_effects=True),
    )(features.reshape(C, ROWS, COLS), grad_out.reshape(C, ROWS, COLS), kernel_one, kernel_two)
    taps = jax.ShapeDtypeStruct((3, 3, C, C), F32)
    gf, g1, g2 = pl.pallas_call(
        output_kernel,
        out_shape=(jax.ShapeDtypeStruct((C, ROWS, COLS), BF16), taps, taps),
        in_specs=[anywhere] * 2,
        out_specs=(anywhere,) * 3,
        scratch_shapes=[
            pltpu.VMEM((C, ROWS, COLS), BF16),
            pltpu.VMEM((2, plane // 2, chunk, LANES), F32),
            pltpu.VMEM((2, 9 * C * C // LANES, LANES), F32),
            pltpu.VMEM((2, 3, 3, C, C), F32),
            dma((5,)), dma((6,)),
        ],
    )(gf, sums)
    return gf.reshape(features.shape), g1, g2


def solution(mesh, near_row=4, near_col=4):
    return jax.shard_map(
        functools.partial(shards, near_row, near_col),
        mesh=mesh,
        in_specs=(P("dp", None, "row", "col"), P("dp", None, "row", "col"), P(), P()),
        out_specs=(P("dp", None, "row", "col"), P(), P()),
        check_vma=False,
    )
```

```python
import functools

import jax
import jax.numpy as jnp
from jax import lax
from jax.experimental import pallas as pl
from jax.experimental.pallas import tpu as pltpu
from jax.sharding import PartitionSpec as P

MESH = pl.DeviceIdType.MESH
F32, BF16 = jnp.float32, jnp.bfloat16

C = 64
ROWS, COLS = 16, 256
REACH = 4
TALL = ROWS + 2 * REACH
WIDE = 3 * C
LANES = 128
GROUP = 4
SPAN = 6
NEARER = ((0, 2), (1, 1), (1, 3), (0, 1), (0, 3), (1, 0), (3, 0), (0, 0))


def rounded(value):
    return value.astype(BF16).astype(F32)


def sigmoid(value):
    return 0.5 * jnp.tanh(0.5 * value) + 0.5


def spun(value, by):
    return pltpu.roll(value, by % LANES, 1) if by % LANES else value


def dot(a, b):
    return jnp.dot(a, b, preferred_element_type=F32)


def fused_kernel(
    near_row, near_col,
    feat_ref, grad_ref, k1_ref, k2_ref,
    gf_ref, sums_ref,
    raw, taps, feat, grad, sides, side_in, corners, corner_in, weights, x3, h3, e3, d3, prod, slope,
    delta_two, delta_one, edges, gf_rows, gf_raw, total, packed,
    mine, landed, part, stacked, final, gathered,
    in_sem, out_sem, sum_sem, halo_send, halo_recv,
    scatter_send, scatter_recv, depth_send, depth_recv, gather_send, gather_recv,
):
    dp, row, col = lax.axis_index("dp"), lax.axis_index("row"), lax.axis_index("col")
    n_dp, n_row, n_col = lax.axis_size("dp"), lax.axis_size("row"), lax.axis_size("col")
    plane = n_dp * near_row * near_col
    far_rows = n_row // near_row
    depth = far_rows * (n_col // near_col)
    far_row, far_col = row // near_row, col // near_col
    me = (dp * near_row + row % near_row) * near_col + col % near_col
    layer = far_col * far_rows + far_row

    def in_depth(step):
        other = (layer + step) % depth
        return (
            dp,
            other % far_rows * near_row + row % near_row,
            other // far_rows * near_col + col % near_col,
        )

    def hops(step, size):
        return min(step, size - step)

    cores = [(dp + i) % n_dp for i in range(n_dp)]
    near_rows = [(row % near_row + i) % near_row for i in range(near_row)]
    near_cols = [(col % near_col + i) % near_col for i in range(near_col)]
    offsets = [(i, j, k) for i in range(n_dp) for j in range(near_row) for k in range(near_col)][1:]
    offsets.sort(key=lambda at: -hops(at[1], near_row) - hops(at[2], near_col))
    def chunk_of(core, y, x):
        return (core * (near_row // 2) + y % (near_row // 2)) * near_col + (x + y // (near_row // 2) * (near_col // 2)) % near_col

    def peer(at):
        i, j, k = at
        return (
            chunk_of(cores[i], near_rows[j], near_cols[k]),
            (cores[i], far_row * near_row + near_rows[j], far_col * near_col + near_cols[k]),
        )

    peers = [peer(at) for at in offsets]
    closer = [peer((i, j, k)) for i in range(n_dp) for j, k in NEARER if (i, j, k) != (0, 0, 0)]
    own_chunk = chunk_of(dp, row % near_row, col % near_col)
    above = [in_depth(step) for step in sorted(range(1, depth), key=lambda step: -hops(step, depth))]

    up, down = (row + n_row - 1) % n_row, (row + 1) % n_row
    left, right = (col + n_col - 1) % n_col, (col + 1) % n_col

    loads = [
        pltpu.make_async_copy(src, dst, in_sem.at[i])
        for i, (src, dst) in enumerate(
            [(feat_ref, raw.at[0]), (grad_ref, raw.at[1]), (k1_ref, taps.at[0]), (k2_ref, taps.at[1])]
        )
    ]
    for load in loads:
        load.start()

    barrier = pltpu.get_barrier_semaphore()

    def greet(target):
        pl.semaphore_signal(barrier, inc=1, device_id=target, device_id_type=MESH)

    for target in [
        (dp, up, left), (dp, up, right), (dp, down, left), (dp, down, right),
        (dp, up, col), (dp, down, col), (dp, row, left), (dp, row, right),
    ]:
        greet(target)

    for _, target in peers:
        greet(target)
    for target in above:
        greet(target)

    a = lax.broadcasted_iota(jnp.int32, (ROWS * 16, ROWS * 16), 0)
    b = lax.broadcasted_iota(jnp.int32, (ROWS * 16, ROWS * 16), 1)
    swap = jnp.where(a == b % 16 * 16 + b // 16, 1.0, 0.0).astype(BF16)

    for which, rows_ref, first in ((0, feat, REACH), (1, grad, 2)):
        loads[which].wait()
        for block in range(C // 16):
            cells = raw[which, pl.ds(block * 16, 16)].reshape(ROWS * 16, COLS)
            turned = dot(swap, cells).astype(BF16).reshape(ROWS, 16, COLS)
            rows_ref[pl.ds(first, ROWS), pl.ds(block * 16, 16), :] = turned

    lane = lax.broadcasted_iota(jnp.int32, (C, LANES), 1)
    slim_lane = lax.broadcasted_iota(jnp.int32, (16, LANES), 1)

    for side in range(2):
        tile = jnp.zeros((C, LANES), F32)
        for rows_ref, first, turn in ((feat, REACH, 0), (grad, 2, 64)):
            for r in range(ROWS):
                at = ((r + 8) * 4 + turn) % LANES
                cells = rows_ref[first + r, :, pl.ds(side * LANES, LANES)].astype(F32)
                shift = at if side == 0 else (at + 4) % LANES
                if shift:
                    cells = pltpu.roll(cells, shift, 1)
                tile = jnp.where((lane >= at) & (lane < at + 4), cells, tile)
        sides[side] = tile.astype(BF16)
        for end, start in enumerate((32, 80)):
            both = jnp.where((lane >= start) & (lane < start + 16), tile, pltpu.roll(tile, 80, 1))
            folded = jnp.zeros((16, LANES), F32)
            for part_of in range(4):
                piece = spun(both[part_of * 16 : part_of * 16 + 16], 32 * part_of - start)
                folded = jnp.where(slim_lane // 32 == part_of, piece, folded)
            corners[side, end] = folded.astype(BF16)

    pl.semaphore_wait(barrier, 8 + plane + depth - 2)

    def send(i, src, dst, target):
        return pltpu.make_async_remote_copy(
            src_ref=src, dst_ref=dst, send_sem=halo_send.at[i], recv_sem=halo_recv.at[i],
            device_id=target, device_id_type=MESH,
        )

    side_copies = [
        send(0, sides.at[1], side_in.at[0], (dp, row, right)),
        send(1, sides.at[0], side_in.at[1], (dp, row, left)),
        send(2, corners.at[1, 1], corner_in.at[0], (dp, down, right)),
        send(3, corners.at[1, 0], corner_in.at[1], (dp, up, right)),
        send(4, corners.at[0, 1], corner_in.at[2], (dp, down, left)),
        send(5, corners.at[0, 0], corner_in.at[3], (dp, up, left)),
        send(6, sides, side_in.at[pl.ds(2, 2)], (dp, down, col)),
        send(7, sides, side_in.at[pl.ds(4, 2)], (dp, up, col)),
    ]
    row_copies = [
        send(8, feat.at[pl.ds(REACH, REACH)], feat.at[pl.ds(REACH + ROWS, REACH)], (dp, up, col)),
        send(9, feat.at[pl.ds(ROWS, REACH)], feat.at[pl.ds(0, REACH)], (dp, down, col)),
        send(10, grad.at[pl.ds(2, 2)], grad.at[pl.ds(2 + ROWS, 2)], (dp, up, col)),
        send(11, grad.at[pl.ds(ROWS, 2)], grad.at[pl.ds(0, 2)], (dp, down, col)),
    ]
    for copy in side_copies + row_copies:
        copy.start()

    for i in range(2):
        loads[2 + i].wait()
        for ky in range(3):
            for kx in range(3):
                weights[i, pl.ds(ky * C, C), pl.ds(kx * C, C)] = taps[i, ky, kx]
                flipped = taps[i, 2 - ky, 2 - kx].astype(F32).T.astype(BF16)
                weights[3 - i, pl.ds(ky * C, C), pl.ds(kx * C, C)] = flipped
    for rows_ref in (delta_one, delta_two):
        for r in (0, 1, ROWS + 2, ROWS + 3):
            rows_ref[r] = jnp.zeros((C, COLS), BF16)

    for copy in side_copies:
        copy.wait_recv()

    middle = (lane >= 32) & (lane < 96)

    def half_turn(value):
        return pltpu.roll(value, 64, 1)

    def joined(here, above, below):
        crossed = half_turn(jnp.where(lane < 64, below, above))
        return (
            jnp.where(middle, here, crossed),
            jnp.where(middle, half_turn(here), jnp.where(lane < 64, above, below)),
        )

    def arrived(i):
        return side_in[i].astype(F32)

    def unfolded(i, start):
        folded = corner_in[i].astype(F32)
        both = jnp.concatenate([spun(folded, start - 32 * part_of) for part_of in range(4)], axis=0)
        return jnp.where((lane >= start) & (lane < start + 16), both, pltpu.roll(both, 48, 1))

    groups = [
        joined(arrived(0), unfolded(0, 80), unfolded(1, 32)),
        joined(sides[0].astype(F32), arrived(2), arrived(4)),
        joined(sides[1].astype(F32), arrived(3), arrived(5)),
        joined(arrived(1), unfolded(2, 80), unfolded(3, 32)),
    ]

    spot = lane // 4 - 8
    line = row * ROWS + spot
    on_map = (line >= 0) & (line < n_row * ROWS)
    shown = [
        jnp.where(on_map & ok, 1.0, 0.0)
        for ok in (col > 0, col >= 0, col >= 0, col < n_col - 1)
    ]
    column = lane % 4

    def side_conv(which, tiles):
        a, b, c, d = tiles
        west = [
            pltpu.roll(a, 1, 1), jnp.where(column == 0, pltpu.roll(a, 125, 1), pltpu.roll(b, 1, 1)),
            pltpu.roll(c, 1, 1), jnp.where(column == 0, pltpu.roll(c, 125, 1), pltpu.roll(d, 1, 1)),
        ]
        east = [
            jnp.where(column == 3, pltpu.roll(b, 3, 1), pltpu.roll(a, 127, 1)), pltpu.roll(b, 127, 1),
            jnp.where(column == 3, pltpu.roll(d, 3, 1), pltpu.roll(c, 127, 1)), pltpu.roll(d, 127, 1),
        ]
        stack = jnp.concatenate([jnp.concatenate(part, axis=1) for part in (west, list(tiles), east)], axis=0)
        out = dot(weights[which], stack.astype(BF16))
        return [
            pltpu.roll(out[0:C, at : at + LANES], 4, 1)
            + out[C : 2 * C, at : at + LANES]
            + pltpu.roll(out[2 * C : 3 * C, at : at + LANES], 124, 1)
            for at in range(0, 4 * LANES, LANES)
        ]

    def keep(which, tiles):
        edges[which, 0] = tiles[0]
        edges[which, 1] = tiles[3]

    feat_tiles = [tile * ok for (tile, _), ok in zip(groups, shown)]
    keep(0, feat_tiles)
    pre = side_conv(0, feat_tiles)
    gates = [sigmoid(v) for v in pre]
    hidden_tiles = [rounded(v * s) * ok for v, s, ok in zip(pre, gates, shown)]
    keep(1, hidden_tiles)
    slopes = [s * (1.0 + v * (1.0 - s)) for v, s in zip(pre, gates)]
    def side_rest():
        pre = side_conv(1, hidden_tiles)
        gates = [sigmoid(v) for v in pre]
        tiles = [rounded(g * (s * (1.0 + v * (1.0 - s)))) * ok for v, s, (_, g), ok in zip(pre, gates, groups, shown)]
        keep(2, tiles)
        back = side_conv(2, tiles)
        keep(3, [rounded(v * s) * ok for v, s, ok in zip(back, slopes, shown)])

    def valid(j):
        at = row * ROWS + j - REACH
        return jnp.where((at >= 0) & (at < n_row * ROWS), 1.0, 0.0).astype(F32)

    def own(j):
        return REACH <= j < REACH + ROWS

    def masked(value, j):
        return value if own(j) else value * valid(j)

    def widened(value, which, j):
        base = (j + 4) * 4
        west = pltpu.roll(value, 1, 1)
        east = pltpu.roll(value, COLS - 1, 1)
        first = pltpu.roll(edges[which, 0], 125 - base, 1)
        last = pltpu.roll(edges[which, 1], 127 - base, 1)
        west = jnp.concatenate([jnp.where(lane == 0, first, west[:, :LANES]), west[:, LANES:]], axis=1)
        east = jnp.concatenate([east[:, :LANES], jnp.where(lane == LANES - 1, last, east[:, LANES:])], axis=1)
        return jnp.concatenate([west, value, east], axis=0).astype(BF16)

    def widen_features(group):
        for j in group:
            x3[j] = widened(masked(feat[j].astype(F32), j), 0, j)

    def conv(which, source, reach, finish, prepare=None, gate=None):
        matrix = weights[which]

        def multiply(group):
            for j in group:
                prod[j] = dot(matrix, source[j])

        def complete(group):
            for j in group:
                finish(j, prod[j - 1, 0:C] + prod[j, C : 2 * C] + prod[j + 1, 2 * C : 3 * C])

        first, last = REACH, REACH + ROWS
        groups = [range(at, at + GROUP) for at in range(first, last, GROUP)]
        ready = first + 1
        if prepare:
            prepare(groups[0])
        for i, group in enumerate(groups):
            if prepare and i + 1 < len(groups):
                prepare(groups[i + 1])
            if i:
                complete(range(ready, group[0] - 1))
                ready = max(ready, group[0] - 1)
            multiply(group)
        border = list(range(first - reach, first)) + list(range(last, last + reach))
        if gate:
            complete(range(ready, last - 1))
            gate()
            prepare(border)
            multiply(border)
        else:
            multiply(border)
            complete(range(ready, last - 1))
        complete(range(first - reach + 1, first + 1))
        complete(range(last - 1, last + reach - 1))

    def first_layer(j, value):
        gate = sigmoid(value)
        if TALL - 4 > j - 1 >= 2:
            slope[j] = gate * (1.0 + value * (1.0 - gate))
        h3[j] = widened(masked(rounded(value * gate), j), 1, j)

    def second_layer(j, value):
        gate = sigmoid(value)
        delta = masked(rounded(grad[j - 2].astype(F32) * (gate * (1.0 + value * (1.0 - gate)))), j)
        if own(j):
            delta_two[j - 2] = delta.astype(BF16)
        e3[j] = widened(delta, 2, j)

    def second_back(j, value):
        delta = masked(rounded(value * slope[j]), j)
        if own(j):
            delta_one[j - 2] = delta.astype(BF16)
        d3[j] = widened(delta, 3, j)

    def first_back(j, value):
        gf_rows[j - REACH] = value.astype(BF16)

    def rows_in():
        for copy in row_copies:
            copy.wait_recv()
        side_rest()

    def kernel_grad(which, delta, source):
        for at in range(0, ROWS + 2, SPAN):
            steps = range(at, at + SPAN)
            piece = lax.dot_general(
                jnp.concatenate([delta[s : s + 3].reshape(WIDE, COLS) for s in steps], axis=1),
                jnp.concatenate([source[s + 3] for s in steps], axis=1),
                (((1,), (1,)), ((), ())), preferred_element_type=F32)
            total[:, 0:WIDE] = piece if at == 0 else total[:, 0:WIDE] + piece
        packed[which, 0:WIDE] = total[:, 0:LANES]
        half = WIDE // 2
        slim = lax.broadcasted_iota(jnp.int32, (half, LANES), 1)
        packed[which, WIDE : WIDE + half] = jnp.where(
            slim < C, total[0:half, LANES : 2 * LANES], pltpu.roll(total[half:WIDE, LANES : 2 * LANES], C, 1))
        chunk = mine.shape[2]
        for j in range(plane // 2):
            mine[which, j] = packed[which, j * chunk : (j + 1) * chunk]

    def scatter(which):
        landed[which, me] = mine[which, own_chunk]
        for other, target in peers:
            pltpu.make_async_remote_copy(
                src_ref=mine.at[which, other], dst_ref=landed.at[which, me],
                send_sem=scatter_send.at[which], recv_sem=scatter_recv.at[which],
                device_id=target, device_id_type=MESH).start()

    def arrivals(which):
        return landed.at[which, pl.ds(0, plane - 1)]

    def exchange(which):
        pltpu.make_async_copy(arrivals(which), arrivals(which), scatter_recv.at[which]).wait()
        part[which] = jnp.sum(landed[which], axis=0)
        stacked[which, layer] = part[which]

        for target in above:
            pltpu.make_async_remote_copy(
                src_ref=part.at[which], dst_ref=stacked.at[which, layer],
                send_sem=depth_send.at[which], recv_sem=depth_recv.at[which],
                device_id=target, device_id_type=MESH).start()

    def others(which):
        return stacked.at[which, pl.ds(0, depth - 1)]

    def members(which):
        return gathered.at[which, pl.ds(0, plane // 2 - 1)]

    def spread(which):
        if depth > 1:
            pltpu.make_async_copy(others(which), others(which), depth_recv.at[which]).wait()
        final[which] = jnp.sum(stacked[which], axis=0) * (1.0 / (n_dp * n_row * ROWS * n_col * COLS) ** 0.5)
        gathered[which, own_chunk] = final[which]

        for _, target in closer:
            pltpu.make_async_remote_copy(
                src_ref=final.at[which], dst_ref=gathered.at[which, own_chunk],
                send_sem=gather_send.at[which], recv_sem=gather_recv.at[which],
                device_id=target, device_id_type=MESH).start()

    def collect(which):
        pltpu.make_async_copy(members(which), members(which), gather_recv.at[which]).wait()
        return pltpu.make_async_copy(gathered.at[which], sums_ref.at[which], sum_sem.at[which])

    conv(0, x3, 4, first_layer, widen_features, rows_in)
    conv(1, h3, 3, second_layer)
    kernel_grad(0, delta_two, h3)
    scatter(0)
    conv(2, e3, 2, second_back)
    kernel_grad(1, delta_one, x3)
    scatter(1)
    exchange(0)
    conv(3, d3, 1, first_back)
    for block in range(C // 16):
        cells = gf_rows[:, pl.ds(block * 16, 16), :].reshape(ROWS * 16, COLS)
        gf_raw[pl.ds(block * 16, 16)] = dot(swap, cells).astype(BF16).reshape(16, ROWS, COLS)
    store = pltpu.make_async_copy(gf_raw, gf_ref, out_sem)
    store.start()
    exchange(1)
    spread(0)
    spread(1)
    stores = [store, collect(0)]
    stores[1].start()
    stores.append(collect(1))
    stores[2].start()
    for store in stores:
        store.wait()
    for copy in side_copies + row_copies:
        copy.wait_send()
    for which in range(2):
        pltpu.make_async_copy(arrivals(which), arrivals(which), scatter_send.at[which]).wait()
        if depth > 1:
            pltpu.make_async_copy(others(which), others(which), depth_send.at[which]).wait()
        pltpu.make_async_copy(members(which), members(which), gather_send.at[which]).wait()


def output_kernel(gf_ref, sums_ref, out_ref, g1_ref, g2_ref, cells, sums, packed, taps, in_sem, out_sem):
    blocks = [pl.ds(at, C // 4) for at in range(0, C, C // 4)]
    sum_load = pltpu.make_async_copy(sums_ref, sums, in_sem.at[4])
    sum_load.start()
    loads = [pltpu.make_async_copy(gf_ref.at[at], cells.at[at], in_sem.at[i]) for i, at in enumerate(blocks)]
    stores = [pltpu.make_async_copy(cells.at[at], out_ref.at[at], out_sem.at[i]) for i, at in enumerate(blocks)]
    for load in loads:
        load.start()
    sum_load.wait()
    chunk = sums.shape[2]
    half = WIDE // 2
    for which, target in ((0, g2_ref), (1, g1_ref)):
        for j in range(sums.shape[1]):
            packed[which, j * chunk : (j + 1) * chunk] = sums[which, j]
        for ky in range(3):
            at = (2 - ky) * C
            for kx in range(2):
                taps[which, ky, kx] = packed[which, at : at + C, kx * C : (kx + 1) * C]
            cut = min(max(half - at, 0), C)
            if cut:
                taps[which, ky, 2, 0:cut] = packed[which, WIDE + at : WIDE + at + cut, 0:C]
            if cut < C:
                start = WIDE + at + cut - half
                taps[which, ky, 2, cut:C] = packed[which, start : start + C - cut, C : 2 * C]
        store = pltpu.make_async_copy(taps.at[which], target, out_sem.at[4 + which])
        store.start()
        stores.append(store)
    for load, store in zip(loads, stores):
        load.wait()
        store.start()
    for store in stores:
        store.wait()


def shards(near_row, near_col, features, grad_out, kernel_one, kernel_two):
    plane = lax.axis_size("dp") * near_row * near_col
    depth = lax.axis_size("row") // near_row * (lax.axis_size("col") // near_col)
    chunk = 9 * C * C // LANES // (plane // 2)
    anywhere = pl.BlockSpec(memory_space=pl.ANY)
    dma = pltpu.SemaphoreType.DMA
    stack = pltpu.VMEM((TALL, WIDE, COLS), BF16)
    gf, sums = pl.pallas_call(
        functools.partial(fused_kernel, near_row, near_col),
        out_shape=(
            jax.ShapeDtypeStruct((C, ROWS, COLS), BF16),
            jax.ShapeDtypeStruct((2, plane // 2, chunk, LANES), F32),
        ),
        in_specs=[anywhere] * 4,
        out_specs=(anywhere, anywhere),
        scratch_shapes=[
            pltpu.VMEM((2, C, ROWS, COLS), BF16),
            pltpu.VMEM((2, 3, 3, C, C), BF16),
            pltpu.VMEM((TALL, C, COLS), BF16),
            pltpu.VMEM((TALL - 4, C, COLS), BF16),
            pltpu.VMEM((2, C, LANES), BF16),
            pltpu.VMEM((6, C, LANES), BF16),
            pltpu.VMEM((2, 2, 16, LANES), BF16),
            pltpu.VMEM((4, 16, LANES), BF16),
            pltpu.VMEM((4, WIDE, WIDE), BF16),
            stack, stack, stack, stack,
            pltpu.VMEM((TALL, WIDE, COLS), F32),
            pltpu.VMEM((TALL, C, COLS), F32),
            pltpu.VMEM((TALL - 4, C, COLS), BF16),
            pltpu.VMEM((TALL - 4, C, COLS), BF16),
            pltpu.VMEM((4, 2, C, LANES), F32),
            pltpu.VMEM((ROWS, C, COLS), BF16),
            pltpu.VMEM((C, ROWS, COLS), BF16),
            pltpu.VMEM((WIDE, COLS), F32),
            pltpu.VMEM((2, 9 * C * C // LANES, LANES), F32),
            pltpu.VMEM((2, plane // 2, chunk, LANES), F32),
            pltpu.VMEM((2, plane, chunk, LANES), F32),
            pltpu.VMEM((2, chunk, LANES), F32),
            pltpu.VMEM((2, depth, chunk, LANES), F32),
            pltpu.VMEM((2, chunk, LANES), F32),
            pltpu.VMEM((2, plane // 2, chunk, LANES), F32),
            dma((4,)), dma, dma((2,)), dma((12,)), dma((12,)),
            dma((2,)), dma((2,)), dma((2,)), dma((2,)), dma((2,)), dma((2,)),
        ],
        compiler_params=pltpu.CompilerParams(collective_id=0, has_side_effects=True),
    )(features.reshape(C, ROWS, COLS), grad_out.reshape(C, ROWS, COLS), kernel_one, kernel_two)
    taps = jax.ShapeDtypeStruct((3, 3, C, C), F32)
    gf, g1, g2 = pl.pallas_call(
        output_kernel,
        out_shape=(jax.ShapeDtypeStruct((C, ROWS, COLS), BF16), taps, taps),
        in_specs=[anywhere] * 2,
        out_specs=(anywhere,) * 3,
        scratch_shapes=[
            pltpu.VMEM((C, ROWS, COLS), BF16),
            pltpu.VMEM((2, plane // 2, chunk, LANES), F32),
            pltpu.VMEM((2, 9 * C * C // LANES, LANES), F32),
            pltpu.VMEM((2, 3, 3, C, C), F32),
            dma((5,)), dma((6,)),
        ],
    )(gf, sums)
    return gf.reshape(features.shape), g1, g2


def solution(mesh, near_row=4, near_col=4):
    return jax.shard_map(
        functools.partial(shards, near_row, near_col),
        mesh=mesh,
        in_specs=(P("dp", None, "row", "col"), P("dp", None, "row", "col"), P(), P()),
        out_specs=(P("dp", None, "row", "col"), P(), P()),
        check_vma=False,
    )
```

```python
import functools

import jax
import jax.numpy as jnp
from jax import lax
from jax.experimental import pallas as pl
from jax.experimental.pallas import tpu as pltpu
from jax.sharding import PartitionSpec as P

MESH = pl.DeviceIdType.MESH
F32, BF16 = jnp.float32, jnp.bfloat16

C = 64
ROWS, COLS = 16, 256
REACH = 4
TALL = ROWS + 2 * REACH
WIDE = 3 * C
LANES = 128
GROUP = 4
SPAN = 6
NEARER = ((0, 2), (1, 1), (1, 3), (0, 1), (0, 3), (1, 0), (3, 0), (0, 0))


def rounded(value):
    return value.astype(BF16).astype(F32)


def sigmoid(value):
    return 0.5 * jnp.tanh(0.5 * value) + 0.5


def spun(value, by):
    return pltpu.roll(value, by % LANES, 1) if by % LANES else value


def dot(a, b):
    return jnp.dot(a, b, preferred_element_type=F32)


def fused_kernel(
    near_row, near_col,
    feat_ref, grad_ref, k1_ref, k2_ref,
    gf_ref, sums_ref,
    raw, taps, feat, grad, sides, side_in, corners, corner_in, weights, x3, h3, e3, d3, prod, slope,
    delta_two, delta_one, edges, gf_rows, gf_raw, total, packed,
    mine, landed, part, stacked, final, gathered,
    in_sem, out_sem, sum_sem, halo_send, halo_recv,
    scatter_send, scatter_recv, depth_send, depth_recv, gather_send, gather_recv,
):
    dp, row, col = lax.axis_index("dp"), lax.axis_index("row"), lax.axis_index("col")
    n_dp, n_row, n_col = lax.axis_size("dp"), lax.axis_size("row"), lax.axis_size("col")
    plane = n_dp * near_row * near_col
    far_rows = n_row // near_row
    depth = far_rows * (n_col // near_col)
    far_row, far_col = row // near_row, col // near_col
    me = (dp * near_row + row % near_row) * near_col + col % near_col
    layer = far_col * far_rows + far_row

    def in_depth(step):
        other = (layer + step) % depth
        return (
            dp,
            other % far_rows * near_row + row % near_row,
            other // far_rows * near_col + col % near_col,
        )

    def hops(step, size):
        return min(step, size - step)

    cores = [(dp + i) % n_dp for i in range(n_dp)]
    near_rows = [(row % near_row + i) % near_row for i in range(near_row)]
    near_cols = [(col % near_col + i) % near_col for i in range(near_col)]
    offsets = [(i, j, k) for i in range(n_dp) for j in range(near_row) for k in range(near_col)][1:]
    offsets.sort(key=lambda at: -hops(at[1], near_row) - hops(at[2], near_col))
    def chunk_of(core, y, x):
        return (core * (near_row // 2) + y % (near_row // 2)) * near_col + (x + y // (near_row // 2) * (near_col // 2)) % near_col

    def peer(at):
        i, j, k = at
        return (
            chunk_of(cores[i], near_rows[j], near_cols[k]),
            (cores[i], far_row * near_row + near_rows[j], far_col * near_col + near_cols[k]),
        )

    peers = [peer(at) for at in offsets]
    closer = [peer((i, j, k)) for i in range(n_dp) for j, k in NEARER if (i, j, k) != (0, 0, 0)]
    own_chunk = chunk_of(dp, row % near_row, col % near_col)
    above = [in_depth(step) for step in sorted(range(1, depth), key=lambda step: -hops(step, depth))]

    up, down = (row + n_row - 1) % n_row, (row + 1) % n_row
    left, right = (col + n_col - 1) % n_col, (col + 1) % n_col

    loads = [
        pltpu.make_async_copy(src, dst, in_sem.at[i])
        for i, (src, dst) in enumerate(
            [(feat_ref, raw.at[0]), (grad_ref, raw.at[1]), (k1_ref, taps.at[0]), (k2_ref, taps.at[1])]
        )
    ]
    for load in loads:
        load.start()

    barrier = pltpu.get_barrier_semaphore()

    def greet(target):
        pl.semaphore_signal(barrier, inc=1, device_id=target, device_id_type=MESH)

    for target in [
        (dp, up, left), (dp, up, right), (dp, down, left), (dp, down, right),
        (dp, up, col), (dp, down, col), (dp, row, left), (dp, row, right),
    ]:
        greet(target)

    for _, target in peers:
        greet(target)
    for target in above:
        greet(target)

    a = lax.broadcasted_iota(jnp.int32, (ROWS * 16, ROWS * 16), 0)
    b = lax.broadcasted_iota(jnp.int32, (ROWS * 16, ROWS * 16), 1)
    swap = jnp.where(a == b % 16 * 16 + b // 16, 1.0, 0.0).astype(BF16)

    for which, rows_ref, first in ((0, feat, REACH), (1, grad, 2)):
        loads[which].wait()
        for block in range(C // 16):
            cells = raw[which, pl.ds(block * 16, 16)].reshape(ROWS * 16, COLS)
            turned = dot(swap, cells).astype(BF16).reshape(ROWS, 16, COLS)
            rows_ref[pl.ds(first, ROWS), pl.ds(block * 16, 16), :] = turned

    lane = lax.broadcasted_iota(jnp.int32, (C, LANES), 1)
    slim_lane = lax.broadcasted_iota(jnp.int32, (16, LANES), 1)

    for side in range(2):
        tile = jnp.zeros((C, LANES), F32)
        for rows_ref, first, turn in ((feat, REACH, 0), (grad, 2, 64)):
            for r in range(ROWS):
                at = ((r + 8) * 4 + turn) % LANES
                cells = rows_ref[first + r, :, pl.ds(side * LANES, LANES)].astype(F32)
                shift = at if side == 0 else (at + 4) % LANES
                if shift:
                    cells = pltpu.roll(cells, shift, 1)
                tile = jnp.where((lane >= at) & (lane < at + 4), cells, tile)
        sides[side] = tile.astype(BF16)
        for end, start in enumerate((32, 80)):
            both = jnp.where((lane >= start) & (lane < start + 16), tile, pltpu.roll(tile, 80, 1))
            folded = jnp.zeros((16, LANES), F32)
            for part_of in range(4):
                piece = spun(both[part_of * 16 : part_of * 16 + 16], 32 * part_of - start)
                folded = jnp.where(slim_lane // 32 == part_of, piece, folded)
            corners[side, end] = folded.astype(BF16)

    pl.semaphore_wait(barrier, 8 + plane + depth - 2)

    def send(i, src, dst, target):
        return pltpu.make_async_remote_copy(
            src_ref=src, dst_ref=dst, send_sem=halo_send.at[i], recv_sem=halo_recv.at[i],
            device_id=target, device_id_type=MESH,
        )

    side_copies = [
        send(0, sides.at[1], side_in.at[0], (dp, row, right)),
        send(1, sides.at[0], side_in.at[1], (dp, row, left)),
        send(2, corners.at[1, 1], corner_in.at[0], (dp, down, right)),
        send(3, corners.at[1, 0], corner_in.at[1], (dp, up, right)),
        send(4, corners.at[0, 1], corner_in.at[2], (dp, down, left)),
        send(5, corners.at[0, 0], corner_in.at[3], (dp, up, left)),
        send(6, sides, side_in.at[pl.ds(2, 2)], (dp, down, col)),
        send(7, sides, side_in.at[pl.ds(4, 2)], (dp, up, col)),
    ]
    row_copies = [
        send(8, feat.at[pl.ds(REACH, REACH)], feat.at[pl.ds(REACH + ROWS, REACH)], (dp, up, col)),
        send(9, feat.at[pl.ds(ROWS, REACH)], feat.at[pl.ds(0, REACH)], (dp, down, col)),
        send(10, grad.at[pl.ds(2, 2)], grad.at[pl.ds(2 + ROWS, 2)], (dp, up, col)),
        send(11, grad.at[pl.ds(ROWS, 2)], grad.at[pl.ds(0, 2)], (dp, down, col)),
    ]
    for copy in side_copies[2:6] + side_copies[:2] + side_copies[6:] + row_copies:
        copy.start()

    for i in range(2):
        loads[2 + i].wait()
        for ky in range(3):
            for kx in range(3):
                weights[i, pl.ds(ky * C, C), pl.ds(kx * C, C)] = taps[i, ky, kx]
                flipped = taps[i, 2 - ky, 2 - kx].astype(F32).T.astype(BF16)
                weights[3 - i, pl.ds(ky * C, C), pl.ds(kx * C, C)] = flipped
    for rows_ref in (delta_one, delta_two):
        for r in (0, 1, ROWS + 2, ROWS + 3):
            rows_ref[r] = jnp.zeros((C, COLS), BF16)

    for copy in side_copies:
        copy.wait_recv()

    middle = (lane >= 32) & (lane < 96)

    def half_turn(value):
        return pltpu.roll(value, 64, 1)

    def joined(here, above, below):
        crossed = half_turn(jnp.where(lane < 64, below, above))
        return (
            jnp.where(middle, here, crossed),
            jnp.where(middle, half_turn(here), jnp.where(lane < 64, above, below)),
        )

    def arrived(i):
        return side_in[i].astype(F32)

    def unfolded(i, start):
        folded = corner_in[i].astype(F32)
        both = jnp.concatenate([spun(folded, start - 32 * part_of) for part_of in range(4)], axis=0)
        return jnp.where((lane >= start) & (lane < start + 16), both, pltpu.roll(both, 48, 1))

    groups = [
        joined(arrived(0), unfolded(0, 80), unfolded(1, 32)),
        joined(sides[0].astype(F32), arrived(2), arrived(4)),
        joined(sides[1].astype(F32), arrived(3), arrived(5)),
        joined(arrived(1), unfolded(2, 80), unfolded(3, 32)),
    ]

    spot = lane // 4 - 8
    line = row * ROWS + spot
    on_map = (line >= 0) & (line < n_row * ROWS)
    shown = [
        jnp.where(on_map & ok, 1.0, 0.0)
        for ok in (col > 0, col >= 0, col >= 0, col < n_col - 1)
    ]
    column = lane % 4

    def side_conv(which, tiles):
        a, b, c, d = tiles
        west = [
            pltpu.roll(a, 1, 1), jnp.where(column == 0, pltpu.roll(a, 125, 1), pltpu.roll(b, 1, 1)),
            pltpu.roll(c, 1, 1), jnp.where(column == 0, pltpu.roll(c, 125, 1), pltpu.roll(d, 1, 1)),
        ]
        east = [
            jnp.where(column == 3, pltpu.roll(b, 3, 1), pltpu.roll(a, 127, 1)), pltpu.roll(b, 127, 1),
            jnp.where(column == 3, pltpu.roll(d, 3, 1), pltpu.roll(c, 127, 1)), pltpu.roll(d, 127, 1),
        ]
        stack = jnp.concatenate([jnp.concatenate(part, axis=1) for part in (west, list(tiles), east)], axis=0)
        out = dot(weights[which], stack.astype(BF16))
        return [
            pltpu.roll(out[0:C, at : at + LANES], 4, 1)
            + out[C : 2 * C, at : at + LANES]
            + pltpu.roll(out[2 * C : 3 * C, at : at + LANES], 124, 1)
            for at in range(0, 4 * LANES, LANES)
        ]

    def keep(which, tiles):
        edges[which, 0] = tiles[0]
        edges[which, 1] = tiles[3]

    feat_tiles = [tile * ok for (tile, _), ok in zip(groups, shown)]
    keep(0, feat_tiles)
    pre = side_conv(0, feat_tiles)
    gates = [sigmoid(v) for v in pre]
    hidden_tiles = [rounded(v * s) * ok for v, s, ok in zip(pre, gates, shown)]
    keep(1, hidden_tiles)
    slopes = [s * (1.0 + v * (1.0 - s)) for v, s in zip(pre, gates)]
    def side_rest():
        pre = side_conv(1, hidden_tiles)
        gates = [sigmoid(v) for v in pre]
        tiles = [rounded(g * (s * (1.0 + v * (1.0 - s)))) * ok for v, s, (_, g), ok in zip(pre, gates, groups, shown)]
        keep(2, tiles)
        back = side_conv(2, tiles)
        keep(3, [rounded(v * s) * ok for v, s, ok in zip(back, slopes, shown)])

    def valid(j):
        at = row * ROWS + j - REACH
        return jnp.where((at >= 0) & (at < n_row * ROWS), 1.0, 0.0).astype(F32)

    def own(j):
        return REACH <= j < REACH + ROWS

    def masked(value, j):
        return value if own(j) else value * valid(j)

    def widened(value, which, j):
        base = (j + 4) * 4
        west = pltpu.roll(value, 1, 1)
        east = pltpu.roll(value, COLS - 1, 1)
        first = pltpu.roll(edges[which, 0], 125 - base, 1)
        last = pltpu.roll(edges[which, 1], 127 - base, 1)
        west = jnp.concatenate([jnp.where(lane == 0, first, west[:, :LANES]), west[:, LANES:]], axis=1)
        east = jnp.concatenate([east[:, :LANES], jnp.where(lane == LANES - 1, last, east[:, LANES:])], axis=1)
        return jnp.concatenate([west, value, east], axis=0).astype(BF16)

    def widen_features(group):
        for j in group:
            x3[j] = widened(masked(feat[j].astype(F32), j), 0, j)

    def conv(which, source, reach, finish, prepare=None, gate=None):
        matrix = weights[which]

        def multiply(group):
            for j in group:
                prod[j] = dot(matrix, source[j])

        def complete(group):
            for j in group:
                finish(j, prod[j - 1, 0:C] + prod[j, C : 2 * C] + prod[j + 1, 2 * C : 3 * C])

        first, last = REACH, REACH + ROWS
        groups = [range(at, at + GROUP) for at in range(first, last, GROUP)]
        ready = first + 1
        if prepare:
            prepare(groups[0])
        for i, group in enumerate(groups):
            if prepare and i + 1 < len(groups):
                prepare(groups[i + 1])
            if i:
                complete(range(ready, group[0] - 1))
                ready = max(ready, group[0] - 1)
            multiply(group)
        border = list(range(first - reach, first)) + list(range(last, last + reach))
        if gate:
            complete(range(ready, last - 1))
            gate()
            prepare(border)
            multiply(border)
        else:
            multiply(border)
            complete(range(ready, last - 1))
        complete(range(first - reach + 1, first + 1))
        complete(range(last - 1, last + reach - 1))

    def first_layer(j, value):
        gate = sigmoid(value)
        if TALL - 4 > j - 1 >= 2:
            slope[j] = gate * (1.0 + value * (1.0 - gate))
        h3[j] = widened(masked(rounded(value * gate), j), 1, j)

    def second_layer(j, value):
        gate = sigmoid(value)
        delta = masked(rounded(grad[j - 2].astype(F32) * (gate * (1.0 + value * (1.0 - gate)))), j)
        if own(j):
            delta_two[j - 2] = delta.astype(BF16)
        e3[j] = widened(delta, 2, j)

    def second_back(j, value):
        delta = masked(rounded(value * slope[j]), j)
        if own(j):
            delta_one[j - 2] = delta.astype(BF16)
        d3[j] = widened(delta, 3, j)

    def first_back(j, value):
        gf_rows[j - REACH] = value.astype(BF16)

    def rows_in():
        for copy in row_copies:
            copy.wait_recv()
        side_rest()

    def kernel_grad(which, delta, source):
        for at in range(0, ROWS + 2, SPAN):
            steps = range(at, at + SPAN)
            piece = lax.dot_general(
                jnp.concatenate([delta[s : s + 3].reshape(WIDE, COLS) for s in steps], axis=1),
                jnp.concatenate([source[s + 3] for s in steps], axis=1),
                (((1,), (1,)), ((), ())), preferred_element_type=F32)
            total[:, 0:WIDE] = piece if at == 0 else total[:, 0:WIDE] + piece
        packed[which, 0:WIDE] = total[:, 0:LANES]
        half = WIDE // 2
        slim = lax.broadcasted_iota(jnp.int32, (half, LANES), 1)
        packed[which, WIDE : WIDE + half] = jnp.where(
            slim < C, total[0:half, LANES : 2 * LANES], pltpu.roll(total[half:WIDE, LANES : 2 * LANES], C, 1))
        chunk = mine.shape[2]
        for j in range(plane // 2):
            mine[which, j] = packed[which, j * chunk : (j + 1) * chunk]

    def scatter(which):
        landed[which, me] = mine[which, own_chunk]
        for other, target in peers:
            pltpu.make_async_remote_copy(
                src_ref=mine.at[which, other], dst_ref=landed.at[which, me],
                send_sem=scatter_send.at[which], recv_sem=scatter_recv.at[which],
                device_id=target, device_id_type=MESH).start()

    def arrivals(which):
        return landed.at[which, pl.ds(0, plane - 1)]

    def exchange(which):
        pltpu.make_async_copy(arrivals(which), arrivals(which), scatter_recv.at[which]).wait()
        part[which] = jnp.sum(landed[which], axis=0)
        stacked[which, layer] = part[which]

        for target in above:
            pltpu.make_async_remote_copy(
                src_ref=part.at[which], dst_ref=stacked.at[which, layer],
                send_sem=depth_send.at[which], recv_sem=depth_recv.at[which],
                device_id=target, device_id_type=MESH).start()

    def others(which):
        return stacked.at[which, pl.ds(0, depth - 1)]

    def members(which):
        return gathered.at[which, pl.ds(0, plane // 2 - 1)]

    def spread(which):
        if depth > 1:
            pltpu.make_async_copy(others(which), others(which), depth_recv.at[which]).wait()
        final[which] = jnp.sum(stacked[which], axis=0) * (1.0 / (n_dp * n_row * ROWS * n_col * COLS) ** 0.5)
        gathered[which, own_chunk] = final[which]

        for _, target in closer:
            pltpu.make_async_remote_copy(
                src_ref=final.at[which], dst_ref=gathered.at[which, own_chunk],
                send_sem=gather_send.at[which], recv_sem=gather_recv.at[which],
                device_id=target, device_id_type=MESH).start()

    def collect(which):
        pltpu.make_async_copy(members(which), members(which), gather_recv.at[which]).wait()
        return pltpu.make_async_copy(gathered.at[which], sums_ref.at[which], sum_sem.at[which])

    conv(0, x3, 4, first_layer, widen_features, rows_in)
    conv(1, h3, 3, second_layer)
    kernel_grad(0, delta_two, h3)
    scatter(0)
    conv(2, e3, 2, second_back)
    kernel_grad(1, delta_one, x3)
    scatter(1)
    conv(3, d3, 1, first_back)
    for block in range(C // 16):
        cells = gf_rows[:, pl.ds(block * 16, 16), :].reshape(ROWS * 16, COLS)
        gf_raw[pl.ds(block * 16, 16)] = dot(swap, cells).astype(BF16).reshape(16, ROWS, COLS)
    store = pltpu.make_async_copy(gf_raw, gf_ref, out_sem)
    store.start()
    exchange(0)
    exchange(1)
    spread(0)
    spread(1)
    stores = [store, collect(0)]
    stores[1].start()
    stores.append(collect(1))
    stores[2].start()
    for store in stores:
        store.wait()
    for copy in side_copies + row_copies:
        copy.wait_send()
    for which in range(2):
        pltpu.make_async_copy(arrivals(which), arrivals(which), scatter_send.at[which]).wait()
        if depth > 1:
            pltpu.make_async_copy(others(which), others(which), depth_send.at[which]).wait()
        pltpu.make_async_copy(members(which), members(which), gather_send.at[which]).wait()


def output_kernel(gf_ref, sums_ref, out_ref, g1_ref, g2_ref, cells, sums, packed, taps, in_sem, out_sem):
    blocks = [pl.ds(at, C // 4) for at in range(0, C, C // 4)]
    sum_load = pltpu.make_async_copy(sums_ref, sums, in_sem.at[4])
    sum_load.start()
    loads = [pltpu.make_async_copy(gf_ref.at[at], cells.at[at], in_sem.at[i]) for i, at in enumerate(blocks)]
    stores = [pltpu.make_async_copy(cells.at[at], out_ref.at[at], out_sem.at[i]) for i, at in enumerate(blocks)]
    for load in loads:
        load.start()
    for load, store in zip(loads, stores):
        load.wait()
        store.start()
    sum_load.wait()
    chunk = sums.shape[2]
    half = WIDE // 2
    for which, target in ((0, g2_ref), (1, g1_ref)):
        for j in range(sums.shape[1]):
            packed[which, j * chunk : (j + 1) * chunk] = sums[which, j]
        for ky in range(3):
            at = (2 - ky) * C
            for kx in range(2):
                taps[which, ky, kx] = packed[which, at : at + C, kx * C : (kx + 1) * C]
            cut = min(max(half - at, 0), C)
            if cut:
                taps[which, ky, 2, 0:cut] = packed[which, WIDE + at : WIDE + at + cut, 0:C]
            if cut < C:
                start = WIDE + at + cut - half
                taps[which, ky, 2, cut:C] = packed[which, start : start + C - cut, C : 2 * C]
        store = pltpu.make_async_copy(taps.at[which], target, out_sem.at[4 + which])
        store.start()
        stores.append(store)
    for store in stores:
        store.wait()


def shards(near_row, near_col, features, grad_out, kernel_one, kernel_two):
    plane = lax.axis_size("dp") * near_row * near_col
    depth = lax.axis_size("row") // near_row * (lax.axis_size("col") // near_col)
    chunk = 9 * C * C // LANES // (plane // 2)
    anywhere = pl.BlockSpec(memory_space=pl.ANY)
    dma = pltpu.SemaphoreType.DMA
    stack = pltpu.VMEM((TALL, WIDE, COLS), BF16)
    gf, sums = pl.pallas_call(
        functools.partial(fused_kernel, near_row, near_col),
        out_shape=(
            jax.ShapeDtypeStruct((C, ROWS, COLS), BF16),
            jax.ShapeDtypeStruct((2, plane // 2, chunk, LANES), F32),
        ),
        in_specs=[anywhere] * 4,
        out_specs=(anywhere, anywhere),
        scratch_shapes=[
            pltpu.VMEM((2, C, ROWS, COLS), BF16),
            pltpu.VMEM((2, 3, 3, C, C), BF16),
            pltpu.VMEM((TALL, C, COLS), BF16),
            pltpu.VMEM((TALL - 4, C, COLS), BF16),
            pltpu.VMEM((2, C, LANES), BF16),
            pltpu.VMEM((6, C, LANES), BF16),
            pltpu.VMEM((2, 2, 16, LANES), BF16),
            pltpu.VMEM((4, 16, LANES), BF16),
            pltpu.VMEM((4, WIDE, WIDE), BF16),
            stack, stack, stack, stack,
            pltpu.VMEM((TALL, WIDE, COLS), F32),
            pltpu.VMEM((TALL, C, COLS), F32),
            pltpu.VMEM((TALL - 4, C, COLS), BF16),
            pltpu.VMEM((TALL - 4, C, COLS), BF16),
            pltpu.VMEM((4, 2, C, LANES), F32),
            pltpu.VMEM((ROWS, C, COLS), BF16),
            pltpu.VMEM((C, ROWS, COLS), BF16),
            pltpu.VMEM((WIDE, COLS), F32),
            pltpu.VMEM((2, 9 * C * C // LANES, LANES), F32),
            pltpu.VMEM((2, plane // 2, chunk, LANES), F32),
            pltpu.VMEM((2, plane, chunk, LANES), F32),
            pltpu.VMEM((2, chunk, LANES), F32),
            pltpu.VMEM((2, depth, chunk, LANES), F32),
            pltpu.VMEM((2, chunk, LANES), F32),
            pltpu.VMEM((2, plane // 2, chunk, LANES), F32),
            dma((4,)), dma, dma((2,)), dma((12,)), dma((12,)),
            dma((2,)), dma((2,)), dma((2,)), dma((2,)), dma((2,)), dma((2,)),
        ],
        compiler_params=pltpu.CompilerParams(collective_id=0, has_side_effects=True),
    )(features.reshape(C, ROWS, COLS), grad_out.reshape(C, ROWS, COLS), kernel_one, kernel_two)
    taps = jax.ShapeDtypeStruct((3, 3, C, C), F32)
    gf, g1, g2 = pl.pallas_call(
        output_kernel,
        out_shape=(jax.ShapeDtypeStruct((C, ROWS, COLS), BF16), taps, taps),
        in_specs=[anywhere] * 2,
        out_specs=(anywhere,) * 3,
        scratch_shapes=[
            pltpu.VMEM((C, ROWS, COLS), BF16),
            pltpu.VMEM((2, plane // 2, chunk, LANES), F32),
            pltpu.VMEM((2, 9 * C * C // LANES, LANES), F32),
            pltpu.VMEM((2, 3, 3, C, C), F32),
            dma((5,)), dma((6,)),
        ],
    )(gf, sums)
    return gf.reshape(features.shape), g1, g2


def solution(mesh, near_row=4, near_col=4):
    return jax.shard_map(
        functools.partial(shards, near_row, near_col),
        mesh=mesh,
        in_specs=(P("dp", None, "row", "col"), P("dp", None, "row", "col"), P(), P()),
        out_specs=(P("dp", None, "row", "col"), P(), P()),
        check_vma=False,
    )
```

```python
import functools

import jax
import jax.numpy as jnp
from jax import lax
from jax.experimental import pallas as pl
from jax.experimental.pallas import tpu as pltpu
from jax.sharding import PartitionSpec as P

MESH = pl.DeviceIdType.MESH
F32, BF16 = jnp.float32, jnp.bfloat16

C = 64
ROWS, COLS = 16, 256
REACH = 4
TALL = ROWS + 2 * REACH
WIDE = 3 * C
LANES = 128
GROUP = 4
SPAN = 6
NEARER = ((0, 2), (1, 1), (1, 3), (0, 1), (0, 3), (1, 0), (3, 0), (0, 0))


def rounded(value):
    return value.astype(BF16).astype(F32)


def sigmoid(value):
    return 0.5 * jnp.tanh(0.5 * value) + 0.5


def spun(value, by):
    return pltpu.roll(value, by % LANES, 1) if by % LANES else value


def dot(a, b):
    return jnp.dot(a, b, preferred_element_type=F32)


def fused_kernel(
    near_row, near_col,
    feat_ref, grad_ref, k1_ref, k2_ref,
    gf_ref, sums_ref,
    raw, taps, feat, grad, sides, side_in, corners, corner_in, weights, x3, h3, e3, d3, prod, slope,
    delta_two, delta_one, edges, gf_rows, gf_raw, total, packed,
    mine, landed, part, stacked, final, gathered,
    in_sem, out_sem, sum_sem, halo_send, halo_recv,
    scatter_send, scatter_recv, depth_send, depth_recv, gather_send, gather_recv,
):
    dp, row, col = lax.axis_index("dp"), lax.axis_index("row"), lax.axis_index("col")
    n_dp, n_row, n_col = lax.axis_size("dp"), lax.axis_size("row"), lax.axis_size("col")
    plane = n_dp * near_row * near_col
    far_rows = n_row // near_row
    depth = far_rows * (n_col // near_col)
    far_row, far_col = row // near_row, col // near_col
    me = (dp * near_row + row % near_row) * near_col + col % near_col
    layer = far_col * far_rows + far_row

    def in_depth(step):
        other = (layer + step) % depth
        return (
            dp,
            other % far_rows * near_row + row % near_row,
            other // far_rows * near_col + col % near_col,
        )

    def hops(step, size):
        return min(step, size - step)

    cores = [(dp + i) % n_dp for i in range(n_dp)]
    near_rows = [(row % near_row + i) % near_row for i in range(near_row)]
    near_cols = [(col % near_col + i) % near_col for i in range(near_col)]
    offsets = [(i, j, k) for i in range(n_dp) for j in range(near_row) for k in range(near_col)][1:]
    offsets.sort(key=lambda at: -hops(at[1], near_row) - hops(at[2], near_col))
    def chunk_of(core, y, x):
        return (core * (near_row // 2) + y % (near_row // 2)) * near_col + (x + y // (near_row // 2) * (near_col // 2)) % near_col

    def peer(at):
        i, j, k = at
        return (
            chunk_of(cores[i], near_rows[j], near_cols[k]),
            (cores[i], far_row * near_row + near_rows[j], far_col * near_col + near_cols[k]),
        )

    peers = [peer(at) for at in offsets]
    closer = [peer((i, j, k)) for i in range(n_dp) for j, k in NEARER if (i, j, k) != (0, 0, 0)]
    own_chunk = chunk_of(dp, row % near_row, col % near_col)
    above = [in_depth(step) for step in sorted(range(1, depth), key=lambda step: -hops(step, depth))]

    up, down = (row + n_row - 1) % n_row, (row + 1) % n_row
    left, right = (col + n_col - 1) % n_col, (col + 1) % n_col

    loads = [
        pltpu.make_async_copy(src, dst, in_sem.at[i])
        for i, (src, dst) in enumerate(
            [(feat_ref, raw.at[0]), (grad_ref, raw.at[1]), (k1_ref, taps.at[0]), (k2_ref, taps.at[1])]
        )
    ]
    for load in loads:
        load.start()

    barrier = pltpu.get_barrier_semaphore()

    def greet(target):
        pl.semaphore_signal(barrier, inc=1, device_id=target, device_id_type=MESH)

    for target in [
        (dp, up, left), (dp, up, right), (dp, down, left), (dp, down, right),
        (dp, up, col), (dp, down, col), (dp, row, left), (dp, row, right),
    ]:
        greet(target)

    for _, target in peers:
        greet(target)
    for target in above:
        greet(target)

    a = lax.broadcasted_iota(jnp.int32, (ROWS * 16, ROWS * 16), 0)
    b = lax.broadcasted_iota(jnp.int32, (ROWS * 16, ROWS * 16), 1)
    swap = jnp.where(a == b % 16 * 16 + b // 16, 1.0, 0.0).astype(BF16)

    for which, rows_ref, first in ((0, feat, REACH), (1, grad, 2)):
        loads[which].wait()
        for block in range(C // 16):
            cells = raw[which, pl.ds(block * 16, 16)].reshape(ROWS * 16, COLS)
            turned = dot(swap, cells).astype(BF16).reshape(ROWS, 16, COLS)
            rows_ref[pl.ds(first, ROWS), pl.ds(block * 16, 16), :] = turned

    lane = lax.broadcasted_iota(jnp.int32, (C, LANES), 1)
    slim_lane = lax.broadcasted_iota(jnp.int32, (16, LANES), 1)

    for side in range(2):
        tile = jnp.zeros((C, LANES), F32)
        for rows_ref, first, turn in ((feat, REACH, 0), (grad, 2, 64)):
            for r in range(ROWS):
                at = ((r + 8) * 4 + turn) % LANES
                cells = rows_ref[first + r, :, pl.ds(side * LANES, LANES)].astype(F32)
                shift = at if side == 0 else (at + 4) % LANES
                if shift:
                    cells = pltpu.roll(cells, shift, 1)
                tile = jnp.where((lane >= at) & (lane < at + 4), cells, tile)
        sides[side] = tile.astype(BF16)
        for end, start in enumerate((32, 80)):
            both = jnp.where((lane >= start) & (lane < start + 16), tile, pltpu.roll(tile, 80, 1))
            folded = jnp.zeros((16, LANES), F32)
            for part_of in range(4):
                piece = spun(both[part_of * 16 : part_of * 16 + 16], 32 * part_of - start)
                folded = jnp.where(slim_lane // 32 == part_of, piece, folded)
            corners[side, end] = folded.astype(BF16)

    pl.semaphore_wait(barrier, 8 + plane + depth - 2)

    def send(i, src, dst, target):
        return pltpu.make_async_remote_copy(
            src_ref=src, dst_ref=dst, send_sem=halo_send.at[i], recv_sem=halo_recv.at[i],
            device_id=target, device_id_type=MESH,
        )

    side_copies = [
        send(0, sides.at[1], side_in.at[0], (dp, row, right)),
        send(1, sides.at[0], side_in.at[1], (dp, row, left)),
        send(2, corners.at[1, 1], corner_in.at[0], (dp, down, right)),
        send(3, corners.at[1, 0], corner_in.at[1], (dp, up, right)),
        send(4, corners.at[0, 1], corner_in.at[2], (dp, down, left)),
        send(5, corners.at[0, 0], corner_in.at[3], (dp, up, left)),
        send(6, sides, side_in.at[pl.ds(2, 2)], (dp, down, col)),
        send(7, sides, side_in.at[pl.ds(4, 2)], (dp, up, col)),
    ]
    row_copies = [
        send(8, feat.at[pl.ds(REACH, REACH)], feat.at[pl.ds(REACH + ROWS, REACH)], (dp, up, col)),
        send(9, feat.at[pl.ds(ROWS, REACH)], feat.at[pl.ds(0, REACH)], (dp, down, col)),
        send(10, grad.at[pl.ds(2, 2)], grad.at[pl.ds(2 + ROWS, 2)], (dp, up, col)),
        send(11, grad.at[pl.ds(ROWS, 2)], grad.at[pl.ds(0, 2)], (dp, down, col)),
    ]
    for copy in side_copies[2:6] + side_copies[:2] + side_copies[6:] + row_copies:
        copy.start()

    for i in range(2):
        loads[2 + i].wait()
        for ky in range(3):
            for kx in range(3):
                weights[i, pl.ds(ky * C, C), pl.ds(kx * C, C)] = taps[i, ky, kx]
                flipped = taps[i, 2 - ky, 2 - kx].astype(F32).T.astype(BF16)
                weights[3 - i, pl.ds(ky * C, C), pl.ds(kx * C, C)] = flipped
    for rows_ref in (delta_one, delta_two):
        for r in (0, 1, ROWS + 2, ROWS + 3):
            rows_ref[r] = jnp.zeros((C, COLS), BF16)

    for copy in side_copies:
        copy.wait_recv()

    middle = (lane >= 32) & (lane < 96)

    def half_turn(value):
        return pltpu.roll(value, 64, 1)

    def joined(here, above, below):
        crossed = half_turn(jnp.where(lane < 64, below, above))
        return (
            jnp.where(middle, here, crossed),
            jnp.where(middle, half_turn(here), jnp.where(lane < 64, above, below)),
        )

    def arrived(i):
        return side_in[i].astype(F32)

    def unfolded(i, start):
        folded = corner_in[i].astype(F32)
        both = jnp.concatenate([spun(folded, start - 32 * part_of) for part_of in range(4)], axis=0)
        return jnp.where((lane >= start) & (lane < start + 16), both, pltpu.roll(both, 48, 1))

    groups = [
        joined(arrived(0), unfolded(0, 80), unfolded(1, 32)),
        joined(sides[0].astype(F32), arrived(2), arrived(4)),
        joined(sides[1].astype(F32), arrived(3), arrived(5)),
        joined(arrived(1), unfolded(2, 80), unfolded(3, 32)),
    ]

    spot = lane // 4 - 8
    line = row * ROWS + spot
    on_map = (line >= 0) & (line < n_row * ROWS)
    shown = [
        jnp.where(on_map & ok, 1.0, 0.0)
        for ok in (col > 0, col >= 0, col >= 0, col < n_col - 1)
    ]
    column = lane % 4

    def side_conv(which, tiles):
        a, b, c, d = tiles
        west = [
            pltpu.roll(a, 1, 1), jnp.where(column == 0, pltpu.roll(a, 125, 1), pltpu.roll(b, 1, 1)),
            pltpu.roll(c, 1, 1), jnp.where(column == 0, pltpu.roll(c, 125, 1), pltpu.roll(d, 1, 1)),
        ]
        east = [
            jnp.where(column == 3, pltpu.roll(b, 3, 1), pltpu.roll(a, 127, 1)), pltpu.roll(b, 127, 1),
            jnp.where(column == 3, pltpu.roll(d, 3, 1), pltpu.roll(c, 127, 1)), pltpu.roll(d, 127, 1),
        ]
        stack = jnp.concatenate([jnp.concatenate(part, axis=1) for part in (west, list(tiles), east)], axis=0)
        out = dot(weights[which], stack.astype(BF16))
        return [
            pltpu.roll(out[0:C, at : at + LANES], 4, 1)
            + out[C : 2 * C, at : at + LANES]
            + pltpu.roll(out[2 * C : 3 * C, at : at + LANES], 124, 1)
            for at in range(0, 4 * LANES, LANES)
        ]

    def keep(which, tiles):
        edges[which, 0] = tiles[0]
        edges[which, 1] = tiles[3]

    feat_tiles = [tile * ok for (tile, _), ok in zip(groups, shown)]
    keep(0, feat_tiles)
    pre = side_conv(0, feat_tiles)
    gates = [sigmoid(v) for v in pre]
    hidden_tiles = [rounded(v * s) * ok for v, s, ok in zip(pre, gates, shown)]
    keep(1, hidden_tiles)
    slopes = [s * (1.0 + v * (1.0 - s)) for v, s in zip(pre, gates)]
    def side_rest():
        pre = side_conv(1, hidden_tiles)
        gates = [sigmoid(v) for v in pre]
        tiles = [rounded(g * (s * (1.0 + v * (1.0 - s)))) * ok for v, s, (_, g), ok in zip(pre, gates, groups, shown)]
        keep(2, tiles)
        back = side_conv(2, tiles)
        keep(3, [rounded(v * s) * ok for v, s, ok in zip(back, slopes, shown)])

    def valid(j):
        at = row * ROWS + j - REACH
        return jnp.where((at >= 0) & (at < n_row * ROWS), 1.0, 0.0).astype(F32)

    def own(j):
        return REACH <= j < REACH + ROWS

    def masked(value, j):
        return value if own(j) else value * valid(j)

    def widened(value, which, j):
        base = (j + 4) * 4
        west = pltpu.roll(value, 1, 1)
        east = pltpu.roll(value, COLS - 1, 1)
        first = pltpu.roll(edges[which, 0], 125 - base, 1)
        last = pltpu.roll(edges[which, 1], 127 - base, 1)
        west = jnp.concatenate([jnp.where(lane == 0, first, west[:, :LANES]), west[:, LANES:]], axis=1)
        east = jnp.concatenate([east[:, :LANES], jnp.where(lane == LANES - 1, last, east[:, LANES:])], axis=1)
        return jnp.concatenate([west, value, east], axis=0).astype(BF16)

    def widen_features(group):
        for j in group:
            x3[j] = widened(masked(feat[j].astype(F32), j), 0, j)

    def conv(which, source, reach, finish, prepare=None, gate=None):
        matrix = weights[which]

        def multiply(group):
            for j in group:
                prod[j] = dot(matrix, source[j])

        def complete(group):
            for j in group:
                finish(j, prod[j - 1, 0:C] + prod[j, C : 2 * C] + prod[j + 1, 2 * C : 3 * C])

        first, last = REACH, REACH + ROWS
        groups = [range(at, at + GROUP) for at in range(first, last, GROUP)]
        ready = first + 1
        if prepare:
            prepare(groups[0])
        for i, group in enumerate(groups):
            if prepare and i + 1 < len(groups):
                prepare(groups[i + 1])
            if i:
                complete(range(ready, group[0] - 1))
                ready = max(ready, group[0] - 1)
            multiply(group)
        border = list(range(first - reach, first)) + list(range(last, last + reach))
        if gate:
            complete(range(ready, last - 1))
            gate()
            prepare(border)
            multiply(border)
        else:
            multiply(border)
            complete(range(ready, last - 1))
        complete(range(first - reach + 1, first + 1))
        complete(range(last - 1, last + reach - 1))

    def first_layer(j, value):
        gate = sigmoid(value)
        if TALL - 4 > j - 1 >= 2:
            slope[j] = gate * (1.0 + value * (1.0 - gate))
        h3[j] = widened(masked(rounded(value * gate), j), 1, j)

    def second_layer(j, value):
        gate = sigmoid(value)
        delta = masked(rounded(grad[j - 2].astype(F32) * (gate * (1.0 + value * (1.0 - gate)))), j)
        if own(j):
            delta_two[j - 2] = delta.astype(BF16)
        e3[j] = widened(delta, 2, j)

    def second_back(j, value):
        delta = masked(rounded(value * slope[j]), j)
        if own(j):
            delta_one[j - 2] = delta.astype(BF16)
        d3[j] = widened(delta, 3, j)

    def first_back(j, value):
        gf_rows[j - REACH] = value.astype(BF16)

    def rows_in():
        for copy in row_copies:
            copy.wait_recv()
        side_rest()

    def kernel_grad(which, delta, source):
        for at in range(0, ROWS + 2, SPAN):
            steps = range(at, at + SPAN)
            piece = lax.dot_general(
                jnp.concatenate([delta[s : s + 3].reshape(WIDE, COLS) for s in steps], axis=1),
                jnp.concatenate([source[s + 3] for s in steps], axis=1),
                (((1,), (1,)), ((), ())), preferred_element_type=F32)
            total[:, 0:WIDE] = piece if at == 0 else total[:, 0:WIDE] + piece
        packed[which, 0:WIDE] = total[:, 0:LANES]
        half = WIDE // 2
        slim = lax.broadcasted_iota(jnp.int32, (half, LANES), 1)
        packed[which, WIDE : WIDE + half] = jnp.where(
            slim < C, total[0:half, LANES : 2 * LANES], pltpu.roll(total[half:WIDE, LANES : 2 * LANES], C, 1))
        chunk = mine.shape[2]
        for j in range(plane // 2):
            mine[which, j] = packed[which, j * chunk : (j + 1) * chunk]

    def scatter(which):
        landed[which, me] = mine[which, own_chunk]
        for other, target in peers:
            pltpu.make_async_remote_copy(
                src_ref=mine.at[which, other], dst_ref=landed.at[which, me],
                send_sem=scatter_send.at[which], recv_sem=scatter_recv.at[which],
                device_id=target, device_id_type=MESH).start()

    def arrivals(which):
        return landed.at[which, pl.ds(0, plane - 1)]

    def exchange(which):
        pltpu.make_async_copy(arrivals(which), arrivals(which), scatter_recv.at[which]).wait()
        part[which] = jnp.sum(landed[which], axis=0).astype(BF16)
        stacked[which, layer] = part[which]

        for target in above:
            pltpu.make_async_remote_copy(
                src_ref=part.at[which], dst_ref=stacked.at[which, layer],
                send_sem=depth_send.at[which], recv_sem=depth_recv.at[which],
                device_id=target, device_id_type=MESH).start()

    def others(which):
        return stacked.at[which, pl.ds(0, depth - 1)]

    def members(which):
        return gathered.at[which, pl.ds(0, plane // 2 - 1)]

    def spread(which):
        if depth > 1:
            pltpu.make_async_copy(others(which), others(which), depth_recv.at[which]).wait()
        final[which] = jnp.sum(stacked[which].astype(F32), axis=0) * (1.0 / (n_dp * n_row * ROWS * n_col * COLS) ** 0.5)
        gathered[which, own_chunk] = final[which]

        for _, target in closer:
            pltpu.make_async_remote_copy(
                src_ref=final.at[which], dst_ref=gathered.at[which, own_chunk],
                send_sem=gather_send.at[which], recv_sem=gather_recv.at[which],
                device_id=target, device_id_type=MESH).start()

    def collect(which):
        pltpu.make_async_copy(members(which), members(which), gather_recv.at[which]).wait()
        return pltpu.make_async_copy(gathered.at[which], sums_ref.at[which], sum_sem.at[which])

    conv(0, x3, 4, first_layer, widen_features, rows_in)
    conv(1, h3, 3, second_layer)
    kernel_grad(0, delta_two, h3)
    scatter(0)
    conv(2, e3, 2, second_back)
    kernel_grad(1, delta_one, x3)
    scatter(1)
    conv(3, d3, 1, first_back)
    for block in range(C // 16):
        cells = gf_rows[:, pl.ds(block * 16, 16), :].reshape(ROWS * 16, COLS)
        gf_raw[pl.ds(block * 16, 16)] = dot(swap, cells).astype(BF16).reshape(16, ROWS, COLS)
    store = pltpu.make_async_copy(gf_raw, gf_ref, out_sem)
    store.start()
    exchange(0)
    exchange(1)
    spread(0)
    spread(1)
    stores = [store, collect(0)]
    stores[1].start()
    stores.append(collect(1))
    stores[2].start()
    for store in stores:
        store.wait()
    for copy in side_copies + row_copies:
        copy.wait_send()
    for which in range(2):
        pltpu.make_async_copy(arrivals(which), arrivals(which), scatter_send.at[which]).wait()
        if depth > 1:
            pltpu.make_async_copy(others(which), others(which), depth_send.at[which]).wait()
        pltpu.make_async_copy(members(which), members(which), gather_send.at[which]).wait()


def output_kernel(gf_ref, sums_ref, out_ref, g1_ref, g2_ref, cells, sums, packed, taps, in_sem, out_sem):
    blocks = [pl.ds(at, C // 4) for at in range(0, C, C // 4)]
    sum_load = pltpu.make_async_copy(sums_ref, sums, in_sem.at[4])
    sum_load.start()
    loads = [pltpu.make_async_copy(gf_ref.at[at], cells.at[at], in_sem.at[i]) for i, at in enumerate(blocks)]
    stores = [pltpu.make_async_copy(cells.at[at], out_ref.at[at], out_sem.at[i]) for i, at in enumerate(blocks)]
    for load in loads:
        load.start()
    for load, store in zip(loads, stores):
        load.wait()
        store.start()
    sum_load.wait()
    chunk = sums.shape[2]
    half = WIDE // 2
    for which, target in ((0, g2_ref), (1, g1_ref)):
        for j in range(sums.shape[1]):
            packed[which, j * chunk : (j + 1) * chunk] = sums[which, j]
        for ky in range(3):
            at = (2 - ky) * C
            for kx in range(2):
                taps[which, ky, kx] = packed[which, at : at + C, kx * C : (kx + 1) * C]
            cut = min(max(half - at, 0), C)
            if cut:
                taps[which, ky, 2, 0:cut] = packed[which, WIDE + at : WIDE + at + cut, 0:C]
            if cut < C:
                start = WIDE + at + cut - half
                taps[which, ky, 2, cut:C] = packed[which, start : start + C - cut, C : 2 * C]
        store = pltpu.make_async_copy(taps.at[which], target, out_sem.at[4 + which])
        store.start()
        stores.append(store)
    for store in stores:
        store.wait()


def shards(near_row, near_col, features, grad_out, kernel_one, kernel_two):
    plane = lax.axis_size("dp") * near_row * near_col
    depth = lax.axis_size("row") // near_row * (lax.axis_size("col") // near_col)
    chunk = 9 * C * C // LANES // (plane // 2)
    anywhere = pl.BlockSpec(memory_space=pl.ANY)
    dma = pltpu.SemaphoreType.DMA
    stack = pltpu.VMEM((TALL, WIDE, COLS), BF16)
    gf, sums = pl.pallas_call(
        functools.partial(fused_kernel, near_row, near_col),
        out_shape=(
            jax.ShapeDtypeStruct((C, ROWS, COLS), BF16),
            jax.ShapeDtypeStruct((2, plane // 2, chunk, LANES), F32),
        ),
        in_specs=[anywhere] * 4,
        out_specs=(anywhere, anywhere),
        scratch_shapes=[
            pltpu.VMEM((2, C, ROWS, COLS), BF16),
            pltpu.VMEM((2, 3, 3, C, C), BF16),
            pltpu.VMEM((TALL, C, COLS), BF16),
            pltpu.VMEM((TALL - 4, C, COLS), BF16),
            pltpu.VMEM((2, C, LANES), BF16),
            pltpu.VMEM((6, C, LANES), BF16),
            pltpu.VMEM((2, 2, 16, LANES), BF16),
            pltpu.VMEM((4, 16, LANES), BF16),
            pltpu.VMEM((4, WIDE, WIDE), BF16),
            stack, stack, stack, stack,
            pltpu.VMEM((TALL, WIDE, COLS), F32),
            pltpu.VMEM((TALL, C, COLS), F32),
            pltpu.VMEM((TALL - 4, C, COLS), BF16),
            pltpu.VMEM((TALL - 4, C, COLS), BF16),
            pltpu.VMEM((4, 2, C, LANES), F32),
            pltpu.VMEM((ROWS, C, COLS), BF16),
            pltpu.VMEM((C, ROWS, COLS), BF16),
            pltpu.VMEM((WIDE, COLS), F32),
            pltpu.VMEM((2, 9 * C * C // LANES, LANES), F32),
            pltpu.VMEM((2, plane // 2, chunk, LANES), F32),
            pltpu.VMEM((2, plane, chunk, LANES), F32),
            pltpu.VMEM((2, chunk, LANES), BF16),
            pltpu.VMEM((2, depth, chunk, LANES), BF16),
            pltpu.VMEM((2, chunk, LANES), F32),
            pltpu.VMEM((2, plane // 2, chunk, LANES), F32),
            dma((4,)), dma, dma((2,)), dma((12,)), dma((12,)),
            dma((2,)), dma((2,)), dma((2,)), dma((2,)), dma((2,)), dma((2,)),
        ],
        compiler_params=pltpu.CompilerParams(collective_id=0, has_side_effects=True),
    )(features.reshape(C, ROWS, COLS), grad_out.reshape(C, ROWS, COLS), kernel_one, kernel_two)
    taps = jax.ShapeDtypeStruct((3, 3, C, C), F32)
    gf, g1, g2 = pl.pallas_call(
        output_kernel,
        out_shape=(jax.ShapeDtypeStruct((C, ROWS, COLS), BF16), taps, taps),
        in_specs=[anywhere] * 2,
        out_specs=(anywhere,) * 3,
        scratch_shapes=[
            pltpu.VMEM((C, ROWS, COLS), BF16),
            pltpu.VMEM((2, plane // 2, chunk, LANES), F32),
            pltpu.VMEM((2, 9 * C * C // LANES, LANES), F32),
            pltpu.VMEM((2, 3, 3, C, C), F32),
            dma((5,)), dma((6,)),
        ],
    )(gf, sums)
    return gf.reshape(features.shape), g1, g2


def solution(mesh, near_row=4, near_col=4):
    return jax.shard_map(
        functools.partial(shards, near_row, near_col),
        mesh=mesh,
        in_specs=(P("dp", None, "row", "col"), P("dp", None, "row", "col"), P(), P()),
        out_specs=(P("dp", None, "row", "col"), P(), P()),
        check_vma=False,
    )
```
